32 devices in a mesh: dp: 4 (over x, core), fsdp: 8 (over z, y).
Axes of the slice: x: 2, y: 2, z: 4, core: 2. Of those that a mesh axis runs over, the one named last changes fastest.
Arguments:
- hidden_in: bfloat16 [32, 512, 1024], P(('dp', 'fsdp')), may hold values from -6 to 6
- value_first: bfloat16 [32, 512, 1024], P(('dp', 'fsdp')), may hold values from -7.5 to 7.5
- segment_ids: int32 [32, 512], P(('dp', 'fsdp')), may hold values from 0 to 3, never falling along the last dimension, each value on 1 to 256 neighbouring positions
- attn_gain: bfloat16 [1024], P('fsdp'), may hold values from 0.5 to 1.5
- w_query: bfloat16 [1024, 1024], P('fsdp'), may hold values from -0.1875 to 0.1875
- w_key: bfloat16 [1024, 1024], P('fsdp'), may hold values from -0.1875 to 0.1875
- w_value: bfloat16 [1024, 1024], P('fsdp'), may hold values from -0.1875 to 0.1875
- w_output: bfloat16 [1024, 1024], P('fsdp'), may hold values from -1.5 to 1.5
- mlp_gain: bfloat16 [1024], P('fsdp'), may hold values from 0.5 to 1.5
- w_gate: bfloat16 [1024, 2816], P('fsdp'), may hold values from -0.1875 to 0.1875
- w_up: bfloat16 [1024, 2816], P('fsdp'), may hold values from -0.1875 to 0.1875
- w_down: bfloat16 [2816, 1024], P('fsdp'), may hold values from -0.21875 to 0.21875
- out_grad: bfloat16 [32, 512, 1024], P(('dp', 'fsdp')), may hold values from -6 to 6
- v1_grad_acc: float32 [32, 512, 1024], P(('dp', 'fsdp')), may hold values from -4 to 4
Outputs:
- block_out: bfloat16 [32, 512, 1024], P(('dp', 'fsdp'))
- input_grad: float32 [32, 512, 1024], P(('dp', 'fsdp'))
- grad_attn_gain: float32 [1024], P('fsdp')
- grad_query: float32 [1024, 1024], P('fsdp')
- grad_key: float32 [1024, 1024], P('fsdp')
- grad_value: float32 [1024, 1024], P('fsdp')
- grad_output: float32 [1024, 1024], P('fsdp')
- grad_mlp_gain: float32 [1024], P('fsdp')
- grad_gate: float32 [1024, 2816], P('fsdp')
- grad_up: float32 [1024, 2816], P('fsdp')
- grad_down: float32 [2816, 1024], P('fsdp')
- v1_grad_out: float32 [32, 512, 1024], P(('dp', 'fsdp'))
- value_norms: float32 [2], replicated
The draws below stay inside these ranges and needn't reach their ends.
All inputs are finite; a program needn't handle non-finite values.
Results may differ from the reference program's by a relative error of at most 0.02.
Values may be sent and summed in bfloat16 or wider, within the bound.
No kernel may reach another device: no remote copies, remote signals or barrier semaphores. Data moves between devices by JAX's collectives and lax.ppermute only.
A program may use at most 192 MiB of HBM per device.

```python
import math
import jax
import jax.numpy as jnp
import numpy as np
from jax import lax

D = 1024
HEADS = 16
HEAD_DIM = 64
FF = 2816
ROW = 512
SEGS = 4
ROWS = 32


def draw_value_first(key, part):
    row_ids = jnp.arange(ROWS, dtype=jnp.float32)
    scales = 0.5 + row_ids / max(ROWS - 1, 1)
    base = jnp.clip(jax.random.normal(key, (ROWS, ROW, D), jnp.float32), -5.0, 5.0)
    return (base * scales[:, None, None]).astype(jnp.bfloat16)


def shard_levels(rng, extent, cuts, low, top_value):
    def one(position, shards_of):
        draws = jax.random.uniform(jax.random.fold_in(jax.random.fold_in(rng, 6), position), (shards_of,), jnp.float32, low / len(cuts), top_value / len(cuts))
        return jnp.repeat(jnp.exp(draws), extent[position] // shards_of).reshape((-1,) + (1,) * (len(extent) - position - 1))

    factor_of = one(*cuts[0])
    for cut in cuts[1:]:
        factor_of = factor_of * one(*cut)
    return factor_of


def profile(amount, total, bound, slope):
    portions = [(1 << 20) // math.isqrt(grade ** slope) + 1 for grade in range(2, amount + 1)]
    spare, holding = total - bound - (amount - 1), [1] * (amount - 1)
    while spare > 0:
        candidates = [i for i in range(amount - 1) if holding[i] < bound]
        pool, remaining = sum([portions[i] for i in candidates]), spare
        for i in candidates:
            more = min(bound - holding[i], max(1, remaining * portions[i] // pool), spare)
            holding[i] = holding[i] + more
            spare = spare - more
    return np.array([bound] + holding)


def uneven(key, number_of, total, reach, slope):
    if number_of == 2:
        one = jax.random.randint(key, (), max(1, total - reach), min(reach, total - 1) + 1)
        return jnp.stack([one, total - one])
    sizes = jnp.asarray(profile(number_of, total, reach, slope), jnp.int32)
    pairs = (number_of - 1) // 2
    giver, receiver = sizes[1:1 + 2 * pairs:2], sizes[2:2 + 2 * pairs:2]
    slack = jnp.minimum(giver - 1, reach - receiver)
    passed = jax.random.randint(jax.random.fold_in(key, 1), (pairs,), 0, 1 << 20) % (slack + 1)
    sizes = sizes.at[1:1 + 2 * pairs:2].set(giver - passed).at[2:2 + 2 * pairs:2].set(receiver + passed)
    return sizes[jax.random.permutation(jax.random.fold_in(key, 2), number_of)]


def scatter_about(own_key, dims, scale, reach, shards=(), kind=jnp.bfloat16):
    result = jax.random.normal(own_key, dims, jnp.float32) * scale
    if len(shards) > 0:
        result = shard_levels(own_key, dims, shards, -0.22, 0.18) * result
    return jnp.clip(result, min=-reach, max=reach).astype(kind)


def setup_inputs(seed: int = 0) -> dict:
    seeds = jax.random.split(jax.random.key(seed), 15)
    return {
        "hidden_in": scatter_about(seeds[0], (ROWS, ROW, D), 1.0, 6.0, ((0, 32),)),
        "value_first": draw_value_first(jax.random.fold_in(seeds[14], 71), 0),
        "segment_ids": jax.vmap(lambda own: jnp.searchsorted(jnp.cumsum(uneven(own, SEGS, ROW, ROW // 2, 1)), jnp.arange(ROW), side="right"))(jax.random.split(seeds[2], ROWS)).reshape((ROWS, ROW)).astype(jnp.int32),
        "attn_gain": jnp.clip(1.0 + 0.1 * jax.random.normal(seeds[3], (D,), jnp.float32), 0.5, 1.5).astype(jnp.bfloat16),
        "w_query": scatter_about(seeds[4], (D, D), D ** -0.5, 0.1875, ((0, 8),)),
        "w_key": scatter_about(seeds[5], (D, D), D ** -0.5, 0.1875, ((0, 8),)),
        "w_value": scatter_about(seeds[6], (D, D), D ** -0.5, 0.1875, ((0, 8),)),
        "w_output": scatter_about(seeds[7], (D, D), (D // 64) ** -0.5, 1.5, ((0, 8),)),
        "mlp_gain": jnp.clip(1.0 + 0.1 * jax.random.normal(seeds[8], (D,), jnp.float32), 0.5, 1.5).astype(jnp.bfloat16),
        "w_gate": scatter_about(seeds[9], (D, FF), D ** -0.5, 0.1875, ((0, 8),)),
        "w_up": scatter_about(seeds[10], (D, FF), D ** -0.5, 0.1875, ((0, 8),)),
        "w_down": scatter_about(seeds[11], (FF, D), (FF // 4) ** -0.5, 0.21875, ((0, 8),)),
        "out_grad": scatter_about(seeds[12], (ROWS, ROW, D), 1.0, 6.0, ((0, 32),)),
        "v1_grad_acc": scatter_about(seeds[13], (ROWS, ROW, D), 0.5, 4.0, ((0, 32),), jnp.float32),
    }


@jax.custom_vjp
def low(v):
    return lax.optimization_barrier(v.astype(jnp.bfloat16)).astype(jnp.float32)

@jax.custom_vjp
def low_back(v):
    return v

def low_keep(v):
    return (low(v), None)

def low_pass(kept, grad):
    return (grad,)

def back_keep(v):
    return (v, None)

def back_low(kept, grad):
    return (low(grad),)
low.defvjp(low_keep, low_pass)
low_back.defvjp(back_keep, back_low)
eps_norm = 1e-06
rope_base = 10000.0
masked_score = -1e+30
highest = lax.Precision.HIGHEST

def positions_of(segment_ids):
    places = lax.broadcasted_iota(jnp.int32, segment_ids.shape, 1)
    before = jnp.concatenate([segment_ids[:, :1] - 1, segment_ids[:, :-1]], axis=1)
    starts = jnp.where(segment_ids != before, places, jnp.zeros_like(places))
    return places - lax.cummax(starts, axis=1)

def rope_tables(positions, half_dim):
    steps_f = jnp.arange(half_dim, dtype=jnp.float32)
    inverse = jnp.exp(steps_f * (-math.log(rope_base) / half_dim))
    angles = positions.astype(jnp.float32)[..., None] * inverse
    return (jnp.cos(angles), jnp.sin(angles))

def rotate(vectors, cosine, sine):
    half_dim = vectors.shape[-1] // 2
    first = vectors[..., :half_dim]
    second = vectors[..., half_dim:]
    cos_b = cosine[..., None, :]
    sin_b = sine[..., None, :]
    return jnp.concatenate([first * cos_b - second * sin_b, second * cos_b + first * sin_b], axis=-1)

def rms_norm(values, gain):
    return values * lax.rsqrt(lax.optimization_barrier(jnp.mean(values * values, axis=-1, keepdims=True)) + eps_norm) * gain

def project(acts, weight):
    return jnp.einsum('brd,de->bre', acts, weight, precision=highest)

def layer_forward(hidden_f, first_f, gain_one, query_w, key_w, value_w, output_w, gain_two, gate_w, up_w, down_w, segs, cosine, sine):
    batch_rows, length = (hidden_f.shape[0], hidden_f.shape[1])
    normed = low(rms_norm(hidden_f, gain_one))
    queries = low_back(project(normed, query_w)).reshape(batch_rows, length, HEADS, HEAD_DIM)
    keys_in = low_back(project(normed, key_w)).reshape(batch_rows, length, HEADS, HEAD_DIM)
    values_own = low_back(project(normed, value_w))
    q_rot = low(rotate(queries, cosine, sine))
    k_rot = low(rotate(keys_in, cosine, sine))
    blended = low(0.5 * values_own + 0.5 * first_f)
    blended_heads = blended.reshape(batch_rows, length, HEADS, HEAD_DIM)
    scores = jnp.einsum('bqhd,bkhd->bhqk', q_rot, k_rot, precision=highest) * HEAD_DIM ** (-0.5)
    scores = low_back(scores)
    places = jnp.arange(length)
    causal = places[None, :] <= places[:, None]
    same_doc = segs[:, :, None] == segs[:, None, :]
    allowed = (causal[None] & same_doc)[:, None]
    scores = jnp.where(allowed, scores, masked_score)
    probs = low(jax.nn.softmax(scores, axis=-1))
    attended = jnp.einsum('bhqk,bkhd->bqhd', probs, blended_heads, precision=highest).reshape(batch_rows, length, D)
    attended = low(low_back(attended))
    mixed = hidden_f + low_back(project(attended, output_w))
    normed_two = low(rms_norm(mixed, gain_two))
    gate = low_back(project(normed_two, gate_w))
    up_val = low_back(project(normed_two, up_w))
    act = low(jax.nn.silu(gate) * up_val)
    out_rows = mixed + low_back(project(act, down_w))
    squares = (jnp.sum(first_f * first_f), jnp.sum(blended * blended))
    return (out_rows, squares)

def reference(hidden_in, value_first, segment_ids, attn_gain, w_query, w_key, w_value, w_output, mlp_gain, w_gate, w_up, w_down, out_grad, v1_grad_acc):
    params = tuple((item.astype(jnp.float32) for item in (attn_gain, w_query, w_key, w_value, w_output, mlp_gain, w_gate, w_up, w_down)))
    group_rows = math.gcd(ROWS, max(1, 4096 // ROW))
    n_groups = ROWS // group_rows

    def split(arr):
        return arr.reshape((n_groups, group_rows) + arr.shape[1:])

    def one_group(running, pieces):
        totals, sums_sq = running
        hidden_g, first_g, segs_g, cot_g = pieces
        cosine, sine = rope_tables(positions_of(segs_g), HEAD_DIM // 2)

        def forward(hidden_f, first_f, *weights):
            return layer_forward(hidden_f, first_f, *weights, segs_g, cosine, sine)
        out_rows, pull, squares = jax.vjp(forward, hidden_g.astype(jnp.float32), first_g.astype(jnp.float32), *params, has_aux=True)
        grads = pull(cot_g.astype(jnp.float32))
        totals = tuple((a_tot + b_new for a_tot, b_new in zip(totals, grads[2:])))
        sums_sq = (sums_sq[0] + squares[0], sums_sq[1] + squares[1])
        return ((totals, sums_sq), (out_rows.astype(jnp.bfloat16), grads[0], grads[1]))
    zero_totals = tuple((jnp.zeros(item.shape, jnp.float32) for item in params))
    zero_sums = (jnp.zeros((), jnp.float32), jnp.zeros((), jnp.float32))
    (totals, sums_sq), (outs, hidden_grads, first_grads) = lax.scan(one_group, (zero_totals, zero_sums), (split(hidden_in), split(value_first), split(segment_ids), split(out_grad)))
    block_out = outs.reshape(ROWS, ROW, D)
    input_grad = hidden_grads.reshape(ROWS, ROW, D)
    v1_grad_out = v1_grad_acc + first_grads.reshape(ROWS, ROW, D)
    count = jnp.float32(ROWS * ROW * D)
    value_norms = jnp.sqrt(jnp.stack([sums_sq[0], sums_sq[1]]) / count)
    return (block_out, input_grad, totals[0], totals[1], totals[2], totals[3], totals[4], totals[5], totals[6], totals[7], totals[8], v1_grad_out, value_norms)
```

```python
import functools
import math

import jax
import jax.numpy as jnp
from jax import lax
from jax.experimental import pallas as pl
from jax.experimental.pallas import tpu as pltpu
from jax.sharding import PartitionSpec as P

HEAD_DIM = 64
LANES = 128
REACH = 256
BLOCK = 128

eps_norm = 1e-06
rope_base = 10000.0
masked_score = -1e30
bf16 = jnp.bfloat16
f32 = jnp.float32


def positions_of(segment_ids):
    places = lax.broadcasted_iota(jnp.int32, segment_ids.shape, 1)
    before = jnp.concatenate([segment_ids[:, :1] - 1, segment_ids[:, :-1]], axis=1)
    starts = jnp.where(segment_ids != before, places, jnp.zeros_like(places))
    return places - lax.cummax(starts, axis=1)


def rope_tables(positions):
    half = HEAD_DIM // 2
    lane = lax.broadcasted_iota(jnp.int32, (1, LANES), 1)
    inverse = jnp.exp((lane % half).astype(f32) * (-math.log(rope_base) / half))
    angles = positions.astype(f32)[:, None] * inverse
    sign = jnp.where(lane % HEAD_DIM < half, -1.0, 1.0).astype(f32)
    return jnp.cos(angles), jnp.sin(angles) * sign


def halves_swapped(u):
    half = HEAD_DIM // 2
    lane = lax.broadcasted_iota(jnp.int32, u.shape, 1)
    return jnp.where(
        lane % HEAD_DIM < half, pltpu.roll(u, LANES - half, 1), pltpu.roll(u, half, 1)
    )


def head_lanes(u, head):
    lane = lax.broadcasted_iota(jnp.int32, u.shape, 1)
    return jnp.where(lane // HEAD_DIM == head, u, jnp.zeros_like(u))


def dot_nt(a, b):
    return lax.dot_general(a, b, (((1,), (1,)), ((), ())), preferred_element_type=f32)


def dot_tn(a, b):
    return lax.dot_general(a, b, (((0,), (0,)), ((), ())), preferred_element_type=f32)


def dot_nn(a, b):
    return jnp.dot(a, b, preferred_element_type=f32)


def softmax_block(q_head, k_rows, begin, first_key, starts):
    scores = dot_nt(q_head, k_rows) * (HEAD_DIM ** (-0.5))
    row = begin + lax.broadcasted_iota(jnp.int32, scores.shape, 0)
    col = first_key + lax.broadcasted_iota(jnp.int32, scores.shape, 1)
    allowed = (col <= row) & (col >= starts)
    scores = jnp.where(allowed, scores, masked_score)
    expo = jnp.exp(scores - jnp.max(scores, axis=1, keepdims=True))
    return expo / jnp.sum(expo, axis=1, keepdims=True)


def key_range(begin):
    return max(0, (begin - REACH + 1) // BLOCK * BLOCK), begin + BLOCK


def attend_kernel(
    start_ref, cos_ref, sin_ref, q_ref, k_ref, v_ref, first_ref,
    out_ref, q_rot_ref, k_rot_ref, blend_ref,
):
    cosine, sine = cos_ref[...], sin_ref[...]
    queries, keys = q_ref[...], k_ref[...]
    q_rot = (queries * cosine + halves_swapped(queries) * sine).astype(bf16)
    k_rot = (keys * cosine + halves_swapped(keys) * sine).astype(bf16)
    blended = (0.5 * v_ref[...] + 0.5 * first_ref[...].astype(f32)).astype(bf16)
    q_rot_ref[...] = q_rot
    k_rot_ref[...] = k_rot
    blend_ref[...] = blended
    for begin in range(0, q_rot.shape[0], BLOCK):
        low, high = key_range(begin)
        starts = start_ref[begin : begin + BLOCK, :]
        total = jnp.zeros((BLOCK, LANES), f32)
        for head in range(LANES // HEAD_DIM):
            q_head = head_lanes(q_rot[begin : begin + BLOCK, :], head)
            probs = softmax_block(q_head, k_rot[low:high, :], begin, low, starts)
            total = total + dot_nn(probs.astype(bf16), head_lanes(blended[low:high, :], head))
        out_ref[begin : begin + BLOCK, :] = total.astype(bf16)


def attend_back_kernel(
    start_ref, cos_ref, sin_ref, q_rot_ref, k_rot_ref, blend_ref, grad_ref,
    dq_ref, dk_ref, dv_ref, dk_sum, dv_sum,
):
    scale = HEAD_DIM ** (-0.5)
    cosine, sine = cos_ref[...], sin_ref[...]
    q_rot, k_rot, blended, grads = q_rot_ref[...], k_rot_ref[...], blend_ref[...], grad_ref[...]
    dk_sum[...] = jnp.zeros_like(dk_sum)
    dv_sum[...] = jnp.zeros_like(dv_sum)
    for begin in range(0, q_rot.shape[0], BLOCK):
        low, high = key_range(begin)
        rows = slice(begin, begin + BLOCK)
        starts = start_ref[rows, :]
        dq = jnp.zeros((BLOCK, LANES), f32)
        for head in range(LANES // HEAD_DIM):
            q_head = head_lanes(q_rot[rows, :], head)
            k_head = head_lanes(k_rot[low:high, :], head)
            g_head = head_lanes(grads[rows, :], head)
            probs = softmax_block(q_head, k_rot[low:high, :], begin, low, starts)
            grad_probs = dot_nt(g_head, blended[low:high, :])
            inner = jnp.sum(probs * grad_probs, axis=1, keepdims=True)
            grad_scores = (probs * (grad_probs - inner)).astype(bf16)
            dq = dq + dot_nn(grad_scores, k_head)
            dk_sum[low:high, :] += dot_tn(grad_scores, q_head)
            dv_sum[low:high, :] += dot_tn(probs.astype(bf16), g_head)
        dq = dq * scale
        dq_ref[rows, :] = (
            dq * cosine[rows, :] - halves_swapped(dq) * sine[rows, :]
        ).astype(bf16)
    dk = dk_sum[...] * scale
    dk_ref[...] = (dk * cosine - halves_swapped(dk) * sine).astype(bf16)
    dv_ref[...] = (0.5 * dv_sum[...]).astype(bf16)


def attend(starts, cosine, sine, qkv, first, length):
    tokens, width = first.shape
    pairs = width // LANES
    per_row = lambda lanes: pl.BlockSpec((length, lanes), lambda r, h: (r, 0))
    part = lambda k: pl.BlockSpec((length, LANES), lambda r, h: (r, k * pairs + h))
    return pl.pallas_call(
        attend_kernel,
        grid=(tokens // length, pairs),
        in_specs=[per_row(1), per_row(LANES), per_row(LANES), part(0), part(1), part(2), part(0)],
        out_specs=[part(0)] * 4,
        out_shape=[jax.ShapeDtypeStruct((tokens, width), bf16)] * 4,
        name="attend",
    )(starts, cosine, sine, qkv, qkv, qkv, first)


def attend_back(starts, cosine, sine, q_rot, k_rot, blended, grads, length):
    tokens, width = grads.shape
    per_row = lambda lanes: pl.BlockSpec((length, lanes), lambda r, h: (r, 0))
    part = pl.BlockSpec((length, LANES), lambda r, h: (r, h))
    return pl.pallas_call(
        attend_back_kernel,
        grid=(tokens // length, width // LANES),
        in_specs=[per_row(1), per_row(LANES), per_row(LANES)] + [part] * 4,
        out_specs=[part] * 3,
        out_shape=[jax.ShapeDtypeStruct((tokens, width), bf16)] * 3,
        scratch_shapes=[pltpu.VMEM((length, LANES), f32)] * 2,
        name="attend_back",
    )(starts, cosine, sine, q_rot, k_rot, blended, grads)


def norm_stats(values):
    return lax.rsqrt(jnp.mean(values * values, axis=-1, keepdims=True) + eps_norm)


def norm_backward(values, inverse, gain_f, grad_out):
    scaled = values * inverse
    grad_scaled = grad_out * gain_f
    grad_gain = jnp.sum(grad_out * scaled, axis=0)
    grad_values = inverse * (
        grad_scaled - scaled * jnp.mean(grad_scaled * scaled, axis=-1, keepdims=True)
    )
    return grad_values, grad_gain


def shards(
    hidden_in, value_first, segment_ids, attn_gain, w_query, w_key, w_value, w_output,
    mlp_gain, w_gate, w_up, w_down, out_grad, v1_grad_acc,
):
    length, width = hidden_in.shape[1:]
    dp, fsdp = lax.axis_size("dp"), lax.axis_size("fsdp")
    core = lax.axis_index("dp") % 2
    hw = width // 2
    ff_half = w_gate.shape[1] // 2

    def swap(values):
        return lax.ppermute(values, "dp", [(i, i ^ 1) for i in range(dp)])

    def other_chip(values):
        total = values
        for step in range(1, dp // 2):
            total = total + lax.ppermute(
                values, "dp", [(i, (i + 2 * step) % dp) for i in range(dp)]
            )
        return total

    def pair(values):
        return jnp.concatenate([values, swap(values)], axis=0)

    def cols(values, which):
        half = values.shape[-1] // 2
        return lax.dynamic_slice_in_dim(values, which * half, half, values.ndim - 1)

    def rows(values, which):
        half = values.shape[0] // 2
        return lax.dynamic_slice_in_dim(values, which * half, half, 0)

    def in_order(mine, other, axis):
        return jnp.concatenate(
            [jnp.where(core == 0, mine, other), jnp.where(core == 0, other, mine)], axis=axis
        )

    def rows_from_cols(mine):
        return in_order(rows(mine, core), swap(rows(mine, 1 - core)), 1)

    def cols_from_rows(mine):
        return in_order(cols(mine, core), swap(cols(mine, 1 - core)), 0)

    def gather(shard):
        return lax.all_gather(shard, "fsdp", axis=0, tiled=True)

    def scatter(whole):
        return lax.psum_scatter(whole, "fsdp", scatter_dimension=0, tiled=True)

    def mine_and_partner(partial):
        return partial[:length] + swap(partial[length:].astype(bf16)).astype(f32)

    gains = jnp.stack([attn_gain, mlp_gain])
    gains = jnp.pad(gains, ((0, w_query.shape[0] - 2), (0, max(0, LANES - gains.shape[1]))))
    shard_a = jnp.concatenate(
        [cols(w, core) for w in (w_query, w_key, w_value, w_output)] + [gains], axis=1
    )
    shard_b = jnp.concatenate([cols(w_gate, core), cols(w_up, core)], axis=1)
    whole_a = gather(shard_a)
    whole_b = gather(shard_b)
    whole_d = gather(cols(w_down, core))
    qkv_mat = whole_a[:, : 3 * hw]
    output_mat = rows_from_cols(whole_a[:, 3 * hw : 4 * hw])
    gain_rows = whole_a[:, 4 * hw :].reshape(fsdp, w_query.shape[0], -1)
    gain_one = gain_rows[:, 0, : attn_gain.shape[0]].reshape(1, width).astype(f32)
    gain_two = gain_rows[:, 1, : attn_gain.shape[0]].reshape(1, width).astype(f32)
    down_mat = rows_from_cols(whole_d)

    segments = pair(segment_ids)
    positions = positions_of(segments)
    starts = (lax.broadcasted_iota(jnp.int32, positions.shape, 1) - positions).reshape(-1, 1)
    cosine, sine = rope_tables(positions.reshape(-1))
    hidden = pair(hidden_in[0]).astype(f32)
    first = value_first[0]
    first_half = jnp.concatenate([cols(first, core), swap(cols(first, 1 - core))], axis=0)
    cotangent = pair(out_grad[0])

    inverse_one = norm_stats(hidden)
    normed = (hidden * inverse_one * gain_one).astype(bf16)
    qkv = dot_nn(normed, qkv_mat)
    attended, q_rot, k_rot, blended = attend(starts, cosine, sine, qkv, first_half, length)
    first_f, blended_f = first.astype(f32), blended.astype(f32)
    square_first, square_blend = jnp.sum(first_f * first_f), jnp.sum(blended_f * blended_f)

    mixed = hidden[:length] + mine_and_partner(dot_nn(attended, output_mat))
    inverse_two = norm_stats(mixed)
    normed_two = pair((mixed * inverse_two * gain_two).astype(bf16))
    gate = dot_nn(normed_two, whole_b[:, :ff_half])
    up_val = dot_nn(normed_two, whole_b[:, ff_half:])
    sigma = jax.nn.sigmoid(gate)
    silu_gate = gate * sigma
    act = (silu_gate * up_val).astype(bf16)
    block_out = (mixed + mine_and_partner(dot_nn(act, down_mat))).astype(bf16)[None]

    grad_down = scatter(cols_from_rows(dot_tn(act, cotangent).astype(bf16)))
    grad_act = dot_nt(cotangent, down_mat)
    grad_gate = (grad_act * up_val * sigma * (1.0 + gate * (1.0 - sigma))).astype(bf16)
    grad_upv = (grad_act * silu_gate).astype(bf16)
    grad_b = scatter(
        jnp.concatenate(
            [dot_tn(normed_two, grad_gate).astype(bf16), dot_tn(normed_two, grad_upv).astype(bf16)],
            axis=1,
        )
    )
    grad_normed_two = mine_and_partner(
        dot_nt(grad_gate, whole_b[:, :ff_half]) + dot_nt(grad_upv, whole_b[:, ff_half:])
    )
    grad_mixed_norm, grad_gain_two = norm_backward(mixed, inverse_two, gain_two, grad_normed_two)
    grad_mixed = out_grad[0].astype(f32) + grad_mixed_norm
    grad_attn = pair(grad_mixed.astype(bf16))
    grad_out_w = cols_from_rows(dot_tn(attended, grad_attn).astype(bf16))
    grad_attended = dot_nt(grad_attn, output_mat).astype(bf16)
    dq, dk, dv = attend_back(starts, cosine, sine, q_rot, k_rot, blended, grad_attended, length)
    grad_a = scatter(
        jnp.concatenate(
            [dot_tn(normed, d).astype(bf16) for d in (dq, dk, dv)] + [grad_out_w], axis=1
        )
    )
    grad_normed = mine_and_partner(
        dot_nt(dq, qkv_mat[:, :hw]) + dot_nt(dk, qkv_mat[:, hw : 2 * hw])
        + dot_nt(dv, qkv_mat[:, 2 * hw :])
    )
    grad_rows_norm, grad_gain_one = norm_backward(
        hidden[:length], inverse_one[:length], gain_one, grad_normed
    )
    input_grad = (grad_mixed + grad_rows_norm)[None]
    grad_first = in_order(dv[:length], swap(dv[length:]), 1)
    v1_grad_out = v1_grad_acc + grad_first.astype(f32)[None]

    small = jnp.concatenate(
        [grad_gain_one, grad_gain_two, jnp.stack([square_first, square_blend])]
    )
    small = lax.psum(small, ("dp", "fsdp"))
    at = lax.axis_index("fsdp") * attn_gain.shape[0]
    share_gain_one = lax.dynamic_slice_in_dim(small[:width], at, attn_gain.shape[0])
    share_gain_two = lax.dynamic_slice_in_dim(small[width : 2 * width], at, attn_gain.shape[0])
    count = f32(dp * fsdp * length * width)
    value_norms = jnp.sqrt(small[2 * width :] / count)

    grad_down = other_chip(grad_down)
    grad_b = other_chip(grad_b)
    grad_a = other_chip(grad_a)

    def whole_columns(mine, other):
        return in_order(mine, other, 1).astype(f32)

    other_down, other_b, other_a = swap(grad_down), swap(grad_b), swap(grad_a)
    share_query, share_key, share_value, share_output = (
        whole_columns(grad_a[:, k * hw : (k + 1) * hw], other_a[:, k * hw : (k + 1) * hw])
        for k in range(4)
    )
    share_gate, share_up = (
        whole_columns(
            grad_b[:, k * ff_half : (k + 1) * ff_half], other_b[:, k * ff_half : (k + 1) * ff_half]
        )
        for k in range(2)
    )
    share_down = whole_columns(grad_down, other_down)
    return (
        block_out, input_grad, share_gain_one, share_query, share_key, share_value, share_output,
        share_gain_two, share_gate, share_up, share_down, v1_grad_out, value_norms,
    )


def solution(mesh):
    tokens = ("dp", "fsdp")
    in_specs = (
        P(tokens, None, None), P(tokens, None, None), P(tokens, None), P("fsdp"),
        P("fsdp", None), P("fsdp", None), P("fsdp", None), P("fsdp", None), P("fsdp"),
        P("fsdp", None), P("fsdp", None), P("fsdp", None), P(tokens, None, None),
        P(tokens, None, None),
    )
    out_specs = (
        P(tokens, None, None), P(tokens, None, None), P("fsdp"), P("fsdp", None),
        P("fsdp", None), P("fsdp", None), P("fsdp", None), P("fsdp"), P("fsdp", None),
        P("fsdp", None), P("fsdp", None), P(tokens, None, None), P(),
    )
    return jax.shard_map(shards, mesh=mesh, in_specs=in_specs, out_specs=out_specs, check_vma=False)
```

```python
import functools
import math

import jax
import jax.numpy as jnp
from jax import lax
from jax.experimental import pallas as pl
from jax.experimental.layout import Layout, with_layout_constraint
from jax.experimental.pallas import tpu as pltpu
from jax.sharding import PartitionSpec as P

HEAD_DIM = 64
LANES = 128
REACH = 256
BLOCK = 128

eps_norm = 1e-06
rope_base = 10000.0
masked_score = -1e30
bf16 = jnp.bfloat16
f32 = jnp.float32


def positions_of(segment_ids):
    places = lax.broadcasted_iota(jnp.int32, segment_ids.shape, 1)
    before = jnp.concatenate([segment_ids[:, :1] - 1, segment_ids[:, :-1]], axis=1)
    starts = jnp.where(segment_ids != before, places, jnp.zeros_like(places))
    return places - lax.cummax(starts, axis=1)


def rope_tables(positions):
    half = HEAD_DIM // 2
    lane = lax.broadcasted_iota(jnp.int32, (1, LANES), 1)
    inverse = jnp.exp((lane % half).astype(f32) * (-math.log(rope_base) / half))
    angles = positions.astype(f32)[:, None] * inverse
    sign = jnp.where(lane % HEAD_DIM < half, -1.0, 1.0).astype(f32)
    return jnp.cos(angles), jnp.sin(angles) * sign


def halves_swapped(u):
    half = HEAD_DIM // 2
    lane = lax.broadcasted_iota(jnp.int32, u.shape, 1)
    return jnp.where(
        lane % HEAD_DIM < half, pltpu.roll(u, LANES - half, 1), pltpu.roll(u, half, 1)
    )


def head_lanes(u, head):
    lane = lax.broadcasted_iota(jnp.int32, u.shape, 1)
    return jnp.where(lane // HEAD_DIM == head, u, jnp.zeros_like(u))


def row_major(values):
    return with_layout_constraint(values, Layout(major_to_minor=(0, 1)))


def dot_nt(a, b):
    return lax.dot_general(a, b, (((1,), (1,)), ((), ())), preferred_element_type=f32)


def dot_tn(a, b):
    return lax.dot_general(a, b, (((0,), (0,)), ((), ())), preferred_element_type=f32)


def dot_nn(a, b):
    return jnp.dot(a, b, preferred_element_type=f32)


def softmax_block(q_head, k_rows, begin, first_key, starts):
    scores = dot_nt(q_head, k_rows) * (HEAD_DIM ** (-0.5))
    row = begin + lax.broadcasted_iota(jnp.int32, scores.shape, 0)
    col = first_key + lax.broadcasted_iota(jnp.int32, scores.shape, 1)
    allowed = (col <= row) & (col >= starts)
    scores = jnp.where(allowed, scores, masked_score)
    expo = jnp.exp(scores - jnp.max(scores, axis=1, keepdims=True))
    return expo / jnp.sum(expo, axis=1, keepdims=True)


def key_range(begin):
    return max(0, (begin - REACH + 1) // BLOCK * BLOCK), begin + BLOCK


def attend_kernel(
    start_ref, cos_ref, sin_ref, q_ref, k_ref, v_ref, first_ref,
    out_ref, q_rot_ref, k_rot_ref, blend_ref,
):
    cosine, sine = cos_ref[...], sin_ref[...]
    queries, keys = q_ref[...], k_ref[...]
    q_rot = (queries * cosine + halves_swapped(queries) * sine).astype(bf16)
    k_rot = (keys * cosine + halves_swapped(keys) * sine).astype(bf16)
    blended = (0.5 * v_ref[...] + 0.5 * first_ref[...].astype(f32)).astype(bf16)
    q_rot_ref[...] = q_rot
    k_rot_ref[...] = k_rot
    blend_ref[...] = blended
    for begin in range(0, q_rot.shape[0], BLOCK):
        low, high = key_range(begin)
        starts = start_ref[begin : begin + BLOCK, :]
        total = jnp.zeros((BLOCK, LANES), f32)
        for head in range(LANES // HEAD_DIM):
            q_head = head_lanes(q_rot[begin : begin + BLOCK, :], head)
            probs = softmax_block(q_head, k_rot[low:high, :], begin, low, starts)
            total = total + dot_nn(probs.astype(bf16), head_lanes(blended[low:high, :], head))
        out_ref[begin : begin + BLOCK, :] = total.astype(bf16)


def attend_back_kernel(
    start_ref, cos_ref, sin_ref, q_rot_ref, k_rot_ref, blend_ref, grad_ref,
    dq_ref, dk_ref, dv_ref, dk_sum, dv_sum,
):
    scale = HEAD_DIM ** (-0.5)
    cosine, sine = cos_ref[...], sin_ref[...]
    q_rot, k_rot, blended, grads = q_rot_ref[...], k_rot_ref[...], blend_ref[...], grad_ref[...]
    dk_sum[...] = jnp.zeros_like(dk_sum)
    dv_sum[...] = jnp.zeros_like(dv_sum)
    for begin in range(0, q_rot.shape[0], BLOCK):
        low, high = key_range(begin)
        rows = slice(begin, begin + BLOCK)
        starts = start_ref[rows, :]
        dq = jnp.zeros((BLOCK, LANES), f32)
        for head in range(LANES // HEAD_DIM):
            q_head = head_lanes(q_rot[rows, :], head)
            k_head = head_lanes(k_rot[low:high, :], head)
            g_head = head_lanes(grads[rows, :], head)
            probs = softmax_block(q_head, k_rot[low:high, :], begin, low, starts)
            grad_probs = dot_nt(g_head, blended[low:high, :])
            inner = jnp.sum(probs * grad_probs, axis=1, keepdims=True)
            grad_scores = (probs * (grad_probs - inner)).astype(bf16)
            dq = dq + dot_nn(grad_scores, k_head)
            dk_sum[low:high, :] += dot_tn(grad_scores, q_head)
            dv_sum[low:high, :] += dot_tn(probs.astype(bf16), g_head)
        dq = dq * scale
        dq_ref[rows, :] = (
            dq * cosine[rows, :] - halves_swapped(dq) * sine[rows, :]
        ).astype(bf16)
    dk = dk_sum[...] * scale
    dk_ref[...] = (dk * cosine - halves_swapped(dk) * sine).astype(bf16)
    dv_ref[...] = (0.5 * dv_sum[...]).astype(bf16)


def attend(starts, cosine, sine, qkv, first, length):
    tokens, width = first.shape
    pairs = width // LANES
    per_row = lambda lanes: pl.BlockSpec((length, lanes), lambda r, h: (r, 0))
    part = lambda k: pl.BlockSpec((length, LANES), lambda r, h: (r, k * pairs + h))
    return pl.pallas_call(
        attend_kernel,
        grid=(tokens // length, pairs),
        in_specs=[per_row(1), per_row(LANES), per_row(LANES), part(0), part(1), part(2), part(0)],
        out_specs=[part(0)] * 4,
        out_shape=[jax.ShapeDtypeStruct((tokens, width), bf16)] * 4,
        name="attend",
    )(starts, cosine, sine, qkv, qkv, qkv, first)


def attend_back(starts, cosine, sine, q_rot, k_rot, blended, grads, length):
    tokens, width = grads.shape
    per_row = lambda lanes: pl.BlockSpec((length, lanes), lambda r, h: (r, 0))
    part = pl.BlockSpec((length, LANES), lambda r, h: (r, h))
    return pl.pallas_call(
        attend_back_kernel,
        grid=(tokens // length, width // LANES),
        in_specs=[per_row(1), per_row(LANES), per_row(LANES)] + [part] * 4,
        out_specs=[part] * 3,
        out_shape=[jax.ShapeDtypeStruct((tokens, width), bf16)] * 3,
        scratch_shapes=[pltpu.VMEM((length, LANES), f32)] * 2,
        name="attend_back",
    )(starts, cosine, sine, q_rot, k_rot, blended, grads)


def order_kernel(at_ref, *refs):
    *pieces, out_ref = refs
    count = len(pieces)
    for step, piece in enumerate(pieces):
        out_ref[lax.rem(at_ref[0] + count - step, count)] = piece[...]


def in_ring_order(place, pieces):
    in_vmem = pl.BlockSpec(memory_space=pltpu.VMEM)
    return pl.pallas_call(
        order_kernel,
        in_specs=[pl.BlockSpec(memory_space=pltpu.SMEM)] + [in_vmem] * len(pieces),
        out_specs=in_vmem,
        out_shape=jax.ShapeDtypeStruct((len(pieces),) + pieces[0].shape, pieces[0].dtype),
        name="ring_order",
    )(jnp.stack([place]), *pieces)


def join_kernel(at_ref, mine_ref, far_ref, other_ref, out_ref):
    size = other_ref.shape[3]
    shared = mine_ref.shape[2] - size
    side, chip = at_ref[0], at_ref[1]
    for from_side, own in enumerate((mine_ref, far_ref)):
        row = side if from_side == 0 else 1 - side
        if shared:
            out_ref[:, row, :, :shared] = own[:, :, :shared]
        for which in range(2):
            @pl.when(chip == which)
            def _():
                first, second = shared + which * size, shared + (1 - which) * size
                out_ref[:, row, :, first : first + size] = own[:, :, shared:]
                out_ref[:, row, :, second : second + size] = other_ref[from_side]


def joined(side, chip, mine, far, other):
    ring, height, held = mine.shape
    in_vmem = pl.BlockSpec(memory_space=pltpu.VMEM)
    full = jax.ShapeDtypeStruct((ring, 2, height, held + other.shape[3]), mine.dtype)
    whole = pl.pallas_call(
        join_kernel,
        in_specs=[pl.BlockSpec(memory_space=pltpu.SMEM)] + [in_vmem] * 3,
        out_specs=in_vmem,
        out_shape=full,
        name="joined",
    )(jnp.stack([side, chip]), mine, far, other)
    return whole.reshape(ring * 2 * height, full.shape[3])


def norm_stats(values):
    return lax.rsqrt(jnp.mean(values * values, axis=-1, keepdims=True) + eps_norm)


def norm_backward(values, inverse, gain_f, grad_out):
    scaled = values * inverse
    grad_scaled = grad_out * gain_f
    grad_gain = jnp.sum(grad_out * scaled, axis=0)
    grad_values = inverse * (
        grad_scaled - scaled * jnp.mean(grad_scaled * scaled, axis=-1, keepdims=True)
    )
    return grad_values, grad_gain


def shards(
    hidden_in, value_first, segment_ids, attn_gain, w_query, w_key, w_value, w_output,
    mlp_gain, w_gate, w_up, w_down, out_grad, v1_grad_acc,
):
    length, width = hidden_in.shape[1:]
    dp, fsdp = lax.axis_size("dp"), lax.axis_size("fsdp")
    core, chip = lax.axis_index("dp") % 2, lax.axis_index("dp") // 2
    chips = dp // 2
    hw = width // 2

    def swap(values):
        return lax.ppermute(values, "dp", [(i, i ^ 1) for i in range(dp)])

    def to_chip(values, step):
        return lax.ppermute(values, "dp", [(i, (i + 2 * step) % dp) for i in range(dp)])

    def part(values, which):
        share = values.shape[-1] // chips
        return lax.dynamic_slice_in_dim(values, which * share, share, values.ndim - 1)

    def chip_parts(values):
        return [part(values, chip)] + [
            to_chip(part(values, (chip + step) % chips), step) for step in range(1, chips)
        ]

    def added(parts):
        return sum(p.astype(f32) for p in parts).astype(bf16)

    def pair(values):
        return jnp.concatenate([values, swap(values)], axis=0)

    def cols(values, which):
        half = values.shape[-1] // 2
        return lax.dynamic_slice_in_dim(values, which * half, half, values.ndim - 1)

    def rows(values, which):
        half = values.shape[0] // 2
        return lax.dynamic_slice_in_dim(values, which * half, half, 0)

    def in_order(mine, other, axis):
        return jnp.concatenate(
            [jnp.where(core == 0, mine, other), jnp.where(core == 0, other, mine)], axis=axis
        )

    def rows_from_cols(mine):
        return in_order(rows(mine, core), swap(rows(mine, 1 - core)), 1)

    def cols_from_rows(mine):
        return in_order(cols(mine, core), swap(cols(mine, 1 - core)), 0)

    def gather(shard):
        return lax.all_gather(shard, "fsdp", axis=0, tiled=True)

    def scatter(whole):
        return lax.psum_scatter(whole, "fsdp", scatter_dimension=0, tiled=True)

    ring, place = fsdp // 2, lax.axis_index("fsdp") // 2
    side = lax.axis_index("fsdp") % 2

    def sides(values):
        return lax.ppermute(values, "fsdp", [(i, i ^ 1) for i in range(fsdp)])

    def around(values, step):
        return lax.ppermute(values, "fsdp", [(i, (i + 2 * step) % fsdp) for i in range(fsdp)])

    def shared_lanes(shard):
        lanes = shard.shape[1] // LANES
        return (lanes - 2 * (lanes * 4 // 11)) * LANES

    def held_columns(shard):
        shared = shared_lanes(shard)
        size = (shard.shape[1] - shared) // 2
        held = lax.dynamic_slice_in_dim(shard, shared + chip * size, size, 1)
        return jnp.concatenate([shard[:, :shared], held], axis=1) if shared else held

    def ring_pieces(held):
        return [held] + [around(held, step) for step in range(1, ring)]

    def swapped_halves(shard, mine, far):
        shared = shared_lanes(shard)
        return jnp.stack([mine[:, :, shared:], far[:, :, shared:]])

    def mine_and_partner(partial):
        return partial[:length] + swap(partial[length:].astype(bf16)).astype(f32)

    gains = jnp.stack([attn_gain, mlp_gain])
    gains = jnp.pad(gains, ((0, w_query.shape[0] - 2), (0, max(0, LANES - gains.shape[1]))))
    by_ring, tie = chips == 2 and fsdp <= 8, lax.optimization_barrier
    shard_a = jnp.concatenate([gains] + [cols(w, core) for w in (w_query, w_key, w_value)], axis=1)
    shard_b = jnp.concatenate([cols(w_output, core), cols(w_gate, core)], axis=1)
    shard_c, shard_d = cols(w_up, core), cols(w_down, core)
    if by_ring:
        join = functools.partial(joined, side, chip)
        pieces_a = ring_pieces(held_columns(shard_a))
        pieces_a, held_b = tie((pieces_a, held_columns(shard_b)))
        pieces_b = ring_pieces(held_b)
        mine_a = in_ring_order(place, pieces_a)
        far_a = sides(mine_a)
        pieces_b, far_a, mine_a, held_c = tie((pieces_b, far_a, mine_a, held_columns(shard_c)))
        pieces_c = ring_pieces(held_c)
        mine_b = in_ring_order(place, pieces_b)
        far_b = sides(mine_b)
        other_a = to_chip(swapped_halves(shard_a, mine_a, far_a), 1)
        pieces_c, far_b, mine_b, other_a, held_d = tie(
            (pieces_c, far_b, mine_b, other_a, held_columns(shard_d))
        )
        pieces_d = ring_pieces(held_d)
        mine_c = in_ring_order(place, pieces_c)
        halves_b = swapped_halves(shard_b, mine_b, far_b)
        mine_c, halves_b, other_a = tie((mine_c, halves_b, other_a))
        far_c, other_b = sides(mine_c), to_chip(halves_b, 1)
        whole_a = join(mine_a, far_a, other_a)
        pieces_d, far_c, mine_c, other_b, whole_a = tie((pieces_d, far_c, mine_c, other_b, whole_a))
        mine_d = in_ring_order(place, pieces_d)
        halves_c = swapped_halves(shard_c, mine_c, far_c)
        mine_d, halves_c, whole_a = tie((mine_d, halves_c, whole_a))
        far_d, other_c = sides(mine_d), to_chip(halves_c, 1)
    else:
        whole_a = gather(shard_a)
    qkv_mat = whole_a[:, gains.shape[1] :]
    gain_rows = whole_a[:, : gains.shape[1]].reshape(fsdp, w_query.shape[0], -1)
    gain_one = gain_rows[:, 0, : attn_gain.shape[0]].reshape(1, width).astype(f32)
    gain_two = gain_rows[:, 1, : attn_gain.shape[0]].reshape(1, width).astype(f32)

    segments = pair(segment_ids)
    positions = positions_of(segments)
    starts = (lax.broadcasted_iota(jnp.int32, positions.shape, 1) - positions).reshape(-1, 1)
    cosine, sine = rope_tables(positions.reshape(-1))
    hidden = pair(hidden_in[0]).astype(f32)
    first = value_first[0]
    first_half = jnp.concatenate([cols(first, core), swap(cols(first, 1 - core))], axis=0)
    cotangent = pair(out_grad[0])

    inverse_one = norm_stats(hidden)
    normed = (hidden * inverse_one * gain_one).astype(bf16)
    qkv = dot_nn(normed, qkv_mat)
    attended, q_rot, k_rot, blended = attend(starts, cosine, sine, qkv, first_half, length)
    if by_ring:
        attended, far_d, other_c = tie((attended, far_d, other_c))
        halves_d = swapped_halves(shard_d, mine_d, far_d)
        halves_d, attended, other_c = tie((halves_d, attended, other_c))
        other_d = to_chip(halves_d, 1)
        whole_b = join(mine_b, far_b, other_b)
    else:
        whole_b = gather(shard_b)
    output_mat, gate_mat = rows_from_cols(whole_b[:, :hw]), whole_b[:, hw:]
    first_f, blended_f = first.astype(f32), blended.astype(f32)
    square_first, square_blend = jnp.sum(first_f * first_f), jnp.sum(blended_f * blended_f)

    mixed = hidden[:length] + mine_and_partner(dot_nn(attended, output_mat))
    inverse_two = norm_stats(mixed)
    normed_two = pair((mixed * inverse_two * gain_two).astype(bf16))
    gate = dot_nn(normed_two, gate_mat)
    up_mat = join(mine_c, far_c, other_c) if by_ring else gather(shard_c)
    up_val = dot_nn(normed_two, up_mat)
    if by_ring:
        other_d, gate, up_val = tie((other_d, gate, up_val))
        whole_d = join(mine_d, far_d, other_d)
    else:
        whole_d = gather(shard_d)
    down_mat = rows_from_cols(whole_d)
    sigma = jax.nn.sigmoid(gate)
    silu_gate = gate * sigma
    act = (silu_gate * up_val).astype(bf16)
    block_out = (mixed + mine_and_partner(dot_nn(act, down_mat))).astype(bf16)[None]

    grad_act = dot_nt(cotangent, down_mat)
    grad_gate = (grad_act * up_val * sigma * (1.0 + gate * (1.0 - sigma))).astype(bf16)
    grad_upv = (grad_act * silu_gate).astype(bf16)
    grad_b = jnp.concatenate(
        [dot_tn(normed_two, grad_gate).astype(bf16), dot_tn(normed_two, grad_upv).astype(bf16)],
        axis=1,
    )
    grad_b, act, grad_gate, grad_upv = tie((grad_b, act, grad_gate, grad_upv))
    grad_b = scatter(grad_b)
    grad_down = chip_parts(cols_from_rows(dot_tn(act, cotangent).astype(bf16)))
    grad_normed_two = mine_and_partner(
        dot_nt(grad_gate, gate_mat) + dot_nt(grad_upv, up_mat)
    )
    grad_mixed_norm, grad_gain_two = norm_backward(mixed, inverse_two, gain_two, grad_normed_two)
    grad_mixed = out_grad[0].astype(f32) + grad_mixed_norm
    grad_attn = pair(grad_mixed.astype(bf16))
    grad_out_w = cols_from_rows(dot_tn(attended, grad_attn).astype(bf16))
    grad_attended = dot_nt(grad_attn, output_mat).astype(bf16)
    grad_out_w = chip_parts(grad_out_w)
    dq, dk, dv = attend_back(starts, cosine, sine, q_rot, k_rot, blended, grad_attended, length)
    grad_down, grad_out_w, dq = tie((grad_down, grad_out_w, dq))
    height, down_height = w_query.shape[0], w_down.shape[0]
    blocks = -(-down_height // height)
    grad_down = added(grad_down).reshape(fsdp, down_height, -1)
    grad_down = jnp.pad(grad_down, ((0, 0), (0, blocks * height - down_height), (0, 0)))
    grad_down = [
        grad_down[:, k * height : (k + 1) * height].reshape(fsdp * height, -1) for k in range(blocks)
    ]
    grad_normed = mine_and_partner(
        dot_nt(dq, qkv_mat[:, :hw]) + dot_nt(dk, qkv_mat[:, hw : 2 * hw])
        + dot_nt(dv, qkv_mat[:, 2 * hw :])
    )
    grad_rows_norm, grad_gain_one = norm_backward(
        hidden[:length], inverse_one[:length], gain_one, grad_normed
    )
    input_grad = (grad_mixed + grad_rows_norm)[None]
    grad_first = in_order(dv[:length], swap(dv[length:]), 1)
    v1_grad_out = v1_grad_acc + grad_first.astype(f32)[None]

    rest = jnp.stack([square_first, square_blend])
    terms = []
    for _ in range(3):
        terms.append(lax.reduce_precision(rest, 8, 7))
        rest = rest - terms[-1]
    terms = jnp.concatenate([jnp.zeros((2,), f32)] + terms)
    row = lax.broadcasted_iota(jnp.int32, (width, 1), 0) % attn_gain.shape[0]
    extra = jnp.concatenate(
        [
            grad_gain_one[:, None], grad_gain_two[:, None],
            jnp.where(row == lax.axis_index("fsdp"), terms[None, 2:], 0.0),
        ],
        axis=1,
    )
    extra = jnp.pad(extra, ((0, 0), (0, LANES - extra.shape[1]))).astype(bf16)
    grad_a = jnp.concatenate(
        [dot_tn(normed, d).astype(bf16) for d in (dq, dk, dv)]
        + [added(grad_out_w)] + grad_down + [extra],
        axis=1,
    )
    grad_a = row_major(scatter(row_major(grad_a)))

    def from_chips(values):
        return [values] + [to_chip(values, step) for step in range(1, chips)]

    def whole_columns(half, other, at, size):
        return in_order(half[:, at : at + size], other[:, at : at + size], 1).astype(f32)

    ff_half, share = gate_mat.shape[1], hw // chips
    half = added(from_chips(grad_b))
    other = swap(half)
    share_gate, share_up = (whole_columns(half, other, k * ff_half, ff_half) for k in range(2))
    got = [row_major(g) for g in from_chips(grad_a)]
    split_at = 3 * hw + (1 + blocks) * share
    by_chip = [
        functools.reduce(
            lambda kept, back: jnp.where(
                (chip - back) % chips == which, got[back][:, 3 * hw : split_at], kept
            ),
            range(1, chips), got[0][:, 3 * hw : split_at],
        )
        for which in range(chips)
    ]
    half = jnp.concatenate(
        [added([g[:, : 3 * hw] for g in got])]
        + [p[:, k * share : (k + 1) * share] for k in range(1 + blocks) for p in by_chip]
        + [g[:, split_at:] for g in got],
        axis=1,
    )
    other = swap(half)
    share_query, share_key, share_value, share_output, *down_blocks = (
        whole_columns(half, other, k * hw, hw) for k in range(4 + blocks)
    )
    share_down = jnp.concatenate(down_blocks, axis=0)[:down_height]
    gain_sums = sum(
        which[:, at : at + LANES].astype(f32)
        for which in (half, other) for at in range((4 + blocks) * hw, half.shape[1], LANES)
    )
    share_gain_one, share_gain_two = gain_sums[:, 0], gain_sums[:, 1]
    squares = jnp.sum(gain_sums[:, 2:8], axis=0).reshape(3, 2).sum(axis=0)
    value_norms = jnp.sqrt(squares / f32(dp * fsdp * length * width))
    return (
        block_out, input_grad, share_gain_one, share_query, share_key, share_value, share_output,
        share_gain_two, share_gate, share_up, share_down, v1_grad_out, value_norms,
    )


def solution(mesh):
    tokens = ("dp", "fsdp")
    in_specs = (
        P(tokens, None, None), P(tokens, None, None), P(tokens, None), P("fsdp"),
        P("fsdp", None), P("fsdp", None), P("fsdp", None), P("fsdp", None), P("fsdp"),
        P("fsdp", None), P("fsdp", None), P("fsdp", None), P(tokens, None, None),
        P(tokens, None, None),
    )
    out_specs = (
        P(tokens, None, None), P(tokens, None, None), P("fsdp"), P("fsdp", None),
        P("fsdp", None), P("fsdp", None), P("fsdp", None), P("fsdp"), P("fsdp", None),
        P("fsdp", None), P("fsdp", None), P(tokens, None, None), P(),
    )
    return jax.shard_map(shards, mesh=mesh, in_specs=in_specs, out_specs=out_specs, check_vma=False)
```

```python
import functools
import math

import jax
import jax.numpy as jnp
from jax import lax
from jax.experimental import pallas as pl
from jax.experimental.layout import Layout, with_layout_constraint
from jax.experimental.pallas import tpu as pltpu
from jax.sharding import PartitionSpec as P

HEAD_DIM = 64
LANES = 128
REACH = 256
BLOCK = 128

eps_norm = 1e-06
rope_base = 10000.0
masked_score = -1e30
bf16 = jnp.bfloat16
f32 = jnp.float32


def positions_of(segment_ids):
    places = lax.broadcasted_iota(jnp.int32, segment_ids.shape, 1)
    before = jnp.concatenate([segment_ids[:, :1] - 1, segment_ids[:, :-1]], axis=1)
    starts = jnp.where(segment_ids != before, places, jnp.zeros_like(places))
    return places - lax.cummax(starts, axis=1)


def rope_tables(positions):
    half = HEAD_DIM // 2
    lane = lax.broadcasted_iota(jnp.int32, (1, LANES), 1)
    inverse = jnp.exp((lane % half).astype(f32) * (-math.log(rope_base) / half))
    angles = positions.astype(f32)[:, None] * inverse
    sign = jnp.where(lane % HEAD_DIM < half, -1.0, 1.0).astype(f32)
    return jnp.cos(angles), jnp.sin(angles) * sign


def halves_swapped(u):
    half = HEAD_DIM // 2
    lane = lax.broadcasted_iota(jnp.int32, u.shape, 1)
    return jnp.where(
        lane % HEAD_DIM < half, pltpu.roll(u, LANES - half, 1), pltpu.roll(u, half, 1)
    )


def head_lanes(u, head):
    lane = lax.broadcasted_iota(jnp.int32, u.shape, 1)
    return jnp.where(lane // HEAD_DIM == head, u, jnp.zeros_like(u))


def row_major(values):
    return with_layout_constraint(values, Layout(major_to_minor=(0, 1)))


def dot_nt(a, b):
    return lax.dot_general(a, b, (((1,), (1,)), ((), ())), preferred_element_type=f32)


def dot_tn(a, b):
    return lax.dot_general(a, b, (((0,), (0,)), ((), ())), preferred_element_type=f32)


def dot_nn(a, b):
    return jnp.dot(a, b, preferred_element_type=f32)


def softmax_block(q_head, k_rows, begin, first_key, starts):
    scores = dot_nt(q_head, k_rows) * (HEAD_DIM ** (-0.5))
    row = begin + lax.broadcasted_iota(jnp.int32, scores.shape, 0)
    col = first_key + lax.broadcasted_iota(jnp.int32, scores.shape, 1)
    allowed = (col <= row) & (col >= starts)
    scores = jnp.where(allowed, scores, masked_score)
    expo = jnp.exp(scores - jnp.max(scores, axis=1, keepdims=True))
    return expo / jnp.sum(expo, axis=1, keepdims=True)


def key_range(begin):
    return max(0, (begin - REACH + 1) // BLOCK * BLOCK), begin + BLOCK


def attend_kernel(
    start_ref, cos_ref, sin_ref, q_ref, k_ref, v_ref, first_ref,
    out_ref, q_rot_ref, k_rot_ref, blend_ref,
):
    cosine, sine = cos_ref[...], sin_ref[...]
    queries, keys = q_ref[...], k_ref[...]
    q_rot = (queries * cosine + halves_swapped(queries) * sine).astype(bf16)
    k_rot = (keys * cosine + halves_swapped(keys) * sine).astype(bf16)
    blended = (0.5 * v_ref[...] + 0.5 * first_ref[...].astype(f32)).astype(bf16)
    q_rot_ref[...] = q_rot
    k_rot_ref[...] = k_rot
    blend_ref[...] = blended
    for begin in range(0, q_rot.shape[0], BLOCK):
        low, high = key_range(begin)
        starts = start_ref[begin : begin + BLOCK, :]
        total = jnp.zeros((BLOCK, LANES), f32)
        for head in range(LANES // HEAD_DIM):
            q_head = head_lanes(q_rot[begin : begin + BLOCK, :], head)
            probs = softmax_block(q_head, k_rot[low:high, :], begin, low, starts)
            total = total + dot_nn(probs.astype(bf16), head_lanes(blended[low:high, :], head))
        out_ref[begin : begin + BLOCK, :] = total.astype(bf16)


def attend_back_kernel(
    start_ref, cos_ref, sin_ref, q_rot_ref, k_rot_ref, blend_ref, grad_ref,
    dq_ref, dk_ref, dv_ref, dk_sum, dv_sum,
):
    scale = HEAD_DIM ** (-0.5)
    cosine, sine = cos_ref[...], sin_ref[...]
    q_rot, k_rot, blended, grads = q_rot_ref[...], k_rot_ref[...], blend_ref[...], grad_ref[...]
    dk_sum[...] = jnp.zeros_like(dk_sum)
    dv_sum[...] = jnp.zeros_like(dv_sum)
    for begin in range(0, q_rot.shape[0], BLOCK):
        low, high = key_range(begin)
        rows = slice(begin, begin + BLOCK)
        starts = start_ref[rows, :]
        dq = jnp.zeros((BLOCK, LANES), f32)
        for head in range(LANES // HEAD_DIM):
            q_head = head_lanes(q_rot[rows, :], head)
            k_head = head_lanes(k_rot[low:high, :], head)
            g_head = head_lanes(grads[rows, :], head)
            probs = softmax_block(q_head, k_rot[low:high, :], begin, low, starts)
            grad_probs = dot_nt(g_head, blended[low:high, :])
            inner = jnp.sum(probs * grad_probs, axis=1, keepdims=True)
            grad_scores = (probs * (grad_probs - inner)).astype(bf16)
            dq = dq + dot_nn(grad_scores, k_head)
            dk_sum[low:high, :] += dot_tn(grad_scores, q_head)
            dv_sum[low:high, :] += dot_tn(probs.astype(bf16), g_head)
        dq = dq * scale
        dq_ref[rows, :] = (
            dq * cosine[rows, :] - halves_swapped(dq) * sine[rows, :]
        ).astype(bf16)
    dk = dk_sum[...] * scale
    dk_ref[...] = (dk * cosine - halves_swapped(dk) * sine).astype(bf16)
    dv_ref[...] = (0.5 * dv_sum[...]).astype(bf16)


def attend(starts, cosine, sine, qkv, first, length):
    tokens, width = first.shape
    pairs = width // LANES
    per_row = lambda lanes: pl.BlockSpec((length, lanes), lambda r, h: (r, 0))
    part = lambda k: pl.BlockSpec((length, LANES), lambda r, h: (r, k * pairs + h))
    return pl.pallas_call(
        attend_kernel,
        grid=(tokens // length, pairs),
        in_specs=[per_row(1), per_row(LANES), per_row(LANES), part(0), part(1), part(2), part(0)],
        out_specs=[part(0)] * 4,
        out_shape=[jax.ShapeDtypeStruct((tokens, width), bf16)] * 4,
        name="attend",
    )(starts, cosine, sine, qkv, qkv, qkv, first)


def attend_back(starts, cosine, sine, q_rot, k_rot, blended, grads, length):
    tokens, width = grads.shape
    per_row = lambda lanes: pl.BlockSpec((length, lanes), lambda r, h: (r, 0))
    part = pl.BlockSpec((length, LANES), lambda r, h: (r, h))
    return pl.pallas_call(
        attend_back_kernel,
        grid=(tokens // length, width // LANES),
        in_specs=[per_row(1), per_row(LANES), per_row(LANES)] + [part] * 4,
        out_specs=[part] * 3,
        out_shape=[jax.ShapeDtypeStruct((tokens, width), bf16)] * 3,
        scratch_shapes=[pltpu.VMEM((length, LANES), f32)] * 2,
        name="attend_back",
    )(starts, cosine, sine, q_rot, k_rot, blended, grads)


def order_kernel(at_ref, *refs):
    *pieces, out_ref = refs
    count = len(pieces)
    for step, piece in enumerate(pieces):
        out_ref[lax.rem(at_ref[0] + count - step, count)] = piece[...]


def in_ring_order(place, pieces):
    in_vmem = pl.BlockSpec(memory_space=pltpu.VMEM)
    return pl.pallas_call(
        order_kernel,
        in_specs=[pl.BlockSpec(memory_space=pltpu.SMEM)] + [in_vmem] * len(pieces),
        out_specs=in_vmem,
        out_shape=jax.ShapeDtypeStruct((len(pieces),) + pieces[0].shape, pieces[0].dtype),
        name="ring_order",
    )(jnp.stack([place]), *pieces)


def join_kernel(at_ref, mine_ref, far_ref, other_ref, out_ref):
    size = other_ref.shape[3]
    shared = mine_ref.shape[2] - size
    side, chip = at_ref[0], at_ref[1]
    for from_side, own in enumerate((mine_ref, far_ref)):
        row = side if from_side == 0 else 1 - side
        if shared:
            out_ref[:, row, :, :shared] = own[:, :, :shared]
        for which in range(2):
            @pl.when(chip == which)
            def _():
                first, second = shared + which * size, shared + (1 - which) * size
                out_ref[:, row, :, first : first + size] = own[:, :, shared:]
                out_ref[:, row, :, second : second + size] = other_ref[from_side]


def joined(side, chip, mine, far, other):
    ring, height, held = mine.shape
    in_vmem = pl.BlockSpec(memory_space=pltpu.VMEM)
    full = jax.ShapeDtypeStruct((ring, 2, height, held + other.shape[3]), mine.dtype)
    whole = pl.pallas_call(
        join_kernel,
        in_specs=[pl.BlockSpec(memory_space=pltpu.SMEM)] + [in_vmem] * 3,
        out_specs=in_vmem,
        out_shape=full,
        name="joined",
    )(jnp.stack([side, chip]), mine, far, other)
    return whole.reshape(ring * 2 * height, full.shape[3])


def norm_stats(values):
    return lax.rsqrt(jnp.mean(values * values, axis=-1, keepdims=True) + eps_norm)


def norm_backward(values, inverse, gain_f, grad_out):
    scaled = values * inverse
    grad_scaled = grad_out * gain_f
    grad_gain = jnp.sum(grad_out * scaled, axis=0)
    grad_values = inverse * (
        grad_scaled - scaled * jnp.mean(grad_scaled * scaled, axis=-1, keepdims=True)
    )
    return grad_values, grad_gain


def shards(
    hidden_in, value_first, segment_ids, attn_gain, w_query, w_key, w_value, w_output,
    mlp_gain, w_gate, w_up, w_down, out_grad, v1_grad_acc,
):
    length, width = hidden_in.shape[1:]
    dp, fsdp = lax.axis_size("dp"), lax.axis_size("fsdp")
    core, chip = lax.axis_index("dp") % 2, lax.axis_index("dp") // 2
    chips = dp // 2
    hw = width // 2

    def swap(values):
        return lax.ppermute(values, "dp", [(i, i ^ 1) for i in range(dp)])

    def to_chip(values, step):
        return lax.ppermute(values, "dp", [(i, (i + 2 * step) % dp) for i in range(dp)])

    def part(values, which):
        share = values.shape[-1] // chips
        return lax.dynamic_slice_in_dim(values, which * share, share, values.ndim - 1)

    def chip_parts(values):
        return [part(values, chip)] + [
            to_chip(part(values, (chip + step) % chips), step) for step in range(1, chips)
        ]

    def added(parts):
        return sum(p.astype(f32) for p in parts).astype(bf16)

    def pair(values):
        return jnp.concatenate([values, swap(values)], axis=0)

    def cols(values, which):
        half = values.shape[-1] // 2
        return lax.dynamic_slice_in_dim(values, which * half, half, values.ndim - 1)

    def rows(values, which):
        half = values.shape[0] // 2
        return lax.dynamic_slice_in_dim(values, which * half, half, 0)

    def in_order(mine, other, axis):
        return jnp.concatenate(
            [jnp.where(core == 0, mine, other), jnp.where(core == 0, other, mine)], axis=axis
        )

    def rows_from_cols(mine):
        return in_order(rows(mine, core), swap(rows(mine, 1 - core)), 1)

    def cols_from_rows(mine):
        return in_order(cols(mine, core), swap(cols(mine, 1 - core)), 0)

    def gather(shard):
        return lax.all_gather(shard, "fsdp", axis=0, tiled=True)

    def scatter(whole):
        return lax.psum_scatter(whole, "fsdp", scatter_dimension=0, tiled=True)

    ring, place = fsdp // 2, lax.axis_index("fsdp") // 2
    side = lax.axis_index("fsdp") % 2

    def sides(values):
        return lax.ppermute(values, "fsdp", [(i, i ^ 1) for i in range(fsdp)])

    def around(values, step):
        return lax.ppermute(values, "fsdp", [(i, (i + 2 * step) % fsdp) for i in range(fsdp)])

    def shared_lanes(shard):
        lanes = shard.shape[1] // LANES
        return (lanes - 2 * (lanes // 2)) * LANES

    def held_columns(shard):
        shared = shared_lanes(shard)
        size = (shard.shape[1] - shared) // 2
        held = lax.dynamic_slice_in_dim(shard, shared + chip * size, size, 1)
        return jnp.concatenate([shard[:, :shared], held], axis=1) if shared else held

    def ring_pieces(held):
        return [held] + [around(held, step) for step in range(1, ring)]

    def swapped_halves(shard, mine, far):
        shared = shared_lanes(shard)
        return jnp.stack([mine[:, :, shared:], far[:, :, shared:]])

    def mine_and_partner(partial):
        return partial[:length] + swap(partial[length:].astype(bf16)).astype(f32)

    gains = jnp.stack([attn_gain, mlp_gain])
    gains = jnp.pad(gains, ((0, w_query.shape[0] - 2), (0, max(0, LANES - gains.shape[1]))))
    by_ring, tie = chips == 2 and fsdp <= 8, lax.optimization_barrier
    shard_a = jnp.concatenate([gains] + [cols(w, core) for w in (w_query, w_key, w_value)], axis=1)
    shard_b = jnp.concatenate([cols(w_output, core), cols(w_gate, core)], axis=1)
    shard_c, shard_d = cols(w_up, core), cols(w_down, core)
    if by_ring:
        join = functools.partial(joined, side, chip)
        pieces_a = ring_pieces(held_columns(shard_a))
        pieces_a, held_b = tie((pieces_a, held_columns(shard_b)))
        pieces_b = ring_pieces(held_b)
        mine_a = in_ring_order(place, pieces_a)
        far_a = sides(mine_a)
        pieces_b, far_a, mine_a, shard_c, shard_d = tie((pieces_b, far_a, mine_a, shard_c, shard_d))
        mine_b = in_ring_order(place, pieces_b)
        halves_a = swapped_halves(shard_a, mine_a, far_a)
        mine_b, halves_a = tie((mine_b, halves_a))
        far_b, other_a = sides(mine_b), to_chip(halves_a, 1)
        far_b, other_a = tie((far_b, other_a))
        halves_b = swapped_halves(shard_b, mine_b, far_b)
        halves_b, other_a = tie((halves_b, other_a))
        other_b = to_chip(halves_b, 1)
        whole_a = join(mine_a, far_a, other_a)
    else:
        whole_a = gather(shard_a)
    up_mat, whole_d = gather(shard_c), gather(shard_d)
    qkv_mat = whole_a[:, gains.shape[1] :]
    gain_rows = whole_a[:, : gains.shape[1]].reshape(fsdp, w_query.shape[0], -1)
    gain_one = gain_rows[:, 0, : attn_gain.shape[0]].reshape(1, width).astype(f32)
    gain_two = gain_rows[:, 1, : attn_gain.shape[0]].reshape(1, width).astype(f32)

    segments = pair(segment_ids)
    positions = positions_of(segments)
    starts = (lax.broadcasted_iota(jnp.int32, positions.shape, 1) - positions).reshape(-1, 1)
    cosine, sine = rope_tables(positions.reshape(-1))
    hidden = pair(hidden_in[0]).astype(f32)
    first = value_first[0]
    first_half = jnp.concatenate([cols(first, core), swap(cols(first, 1 - core))], axis=0)
    cotangent = pair(out_grad[0])

    inverse_one = norm_stats(hidden)
    normed = (hidden * inverse_one * gain_one).astype(bf16)
    qkv = dot_nn(normed, qkv_mat)
    attended, q_rot, k_rot, blended = attend(starts, cosine, sine, qkv, first_half, length)
    if by_ring:
        attended, other_b = tie((attended, other_b))
        whole_b = join(mine_b, far_b, other_b)
    else:
        whole_b = gather(shard_b)
    output_mat, gate_mat = rows_from_cols(whole_b[:, :hw]), whole_b[:, hw:]
    first_f, blended_f = first.astype(f32), blended.astype(f32)
    square_first, square_blend = jnp.sum(first_f * first_f), jnp.sum(blended_f * blended_f)

    mixed = hidden[:length] + mine_and_partner(dot_nn(attended, output_mat))
    inverse_two = norm_stats(mixed)
    normed_two = pair((mixed * inverse_two * gain_two).astype(bf16))
    gate = dot_nn(normed_two, gate_mat)
    up_val = dot_nn(normed_two, up_mat)
    down_mat = rows_from_cols(whole_d)
    sigma = jax.nn.sigmoid(gate)
    silu_gate = gate * sigma
    act = (silu_gate * up_val).astype(bf16)
    block_out = (mixed + mine_and_partner(dot_nn(act, down_mat))).astype(bf16)[None]

    grad_act = dot_nt(cotangent, down_mat)
    grad_gate = (grad_act * up_val * sigma * (1.0 + gate * (1.0 - sigma))).astype(bf16)
    grad_upv = (grad_act * silu_gate).astype(bf16)
    grad_b = jnp.concatenate(
        [dot_tn(normed_two, grad_gate).astype(bf16), dot_tn(normed_two, grad_upv).astype(bf16)],
        axis=1,
    )
    grad_b, act, grad_gate, grad_upv = tie((grad_b, act, grad_gate, grad_upv))
    grad_b = scatter(grad_b)
    grad_down = chip_parts(cols_from_rows(dot_tn(act, cotangent).astype(bf16)))
    grad_normed_two = mine_and_partner(
        dot_nt(grad_gate, gate_mat) + dot_nt(grad_upv, up_mat)
    )
    grad_mixed_norm, grad_gain_two = norm_backward(mixed, inverse_two, gain_two, grad_normed_two)
    grad_mixed = out_grad[0].astype(f32) + grad_mixed_norm
    grad_attn = pair(grad_mixed.astype(bf16))
    grad_out_w = cols_from_rows(dot_tn(attended, grad_attn).astype(bf16))
    grad_attended = dot_nt(grad_attn, output_mat).astype(bf16)
    grad_out_w = chip_parts(grad_out_w)
    dq, dk, dv = attend_back(starts, cosine, sine, q_rot, k_rot, blended, grad_attended, length)
    grad_down, grad_out_w, dq = tie((grad_down, grad_out_w, dq))
    grad_do = jnp.concatenate(
        [added(parts).reshape(fsdp, -1, hw // chips) for parts in (grad_down, grad_out_w)], axis=1
    )
    if by_ring:
        grad_do = grad_do.reshape(ring, 2, *grad_do.shape[1:])
        at_side = lambda which: lax.dynamic_slice_in_dim(grad_do, which, 1, 1)[:, 0]
        do_mine, do_far = at_side(side), at_side(1 - side)
    grad_normed = mine_and_partner(
        dot_nt(dq, qkv_mat[:, :hw]) + dot_nt(dk, qkv_mat[:, hw : 2 * hw])
        + dot_nt(dv, qkv_mat[:, 2 * hw :])
    )
    grad_rows_norm, grad_gain_one = norm_backward(
        hidden[:length], inverse_one[:length], gain_one, grad_normed
    )
    input_grad = (grad_mixed + grad_rows_norm)[None]
    grad_first = in_order(dv[:length], swap(dv[length:]), 1)
    v1_grad_out = v1_grad_acc + grad_first.astype(f32)[None]

    rest = jnp.stack([square_first, square_blend])
    terms = []
    for _ in range(3):
        terms.append(lax.reduce_precision(rest, 8, 7))
        rest = rest - terms[-1]
    terms = jnp.concatenate([jnp.zeros((2,), f32)] + terms)
    row = lax.broadcasted_iota(jnp.int32, (width, 1), 0) % attn_gain.shape[0]
    extra = jnp.concatenate(
        [
            grad_gain_one[:, None], grad_gain_two[:, None],
            jnp.where(row == lax.axis_index("fsdp"), terms[None, 2:], 0.0),
        ],
        axis=1,
    )
    extra = jnp.pad(extra, ((0, 0), (0, LANES - extra.shape[1]))).astype(bf16)
    grad_q, grad_k = (chip_parts(dot_tn(normed, d).astype(bf16)) for d in (dq, dk))
    grad_v = dot_tn(normed, dv).astype(bf16)
    grad_a = jnp.concatenate([added(grad_q), added(grad_k), grad_v, extra], axis=1)
    if by_ring:
        grad_a, grad_b, do_mine, do_far = tie((grad_a, grad_b, do_mine, do_far))
        grad_do = added([do_mine, sides(do_far)])
        at_place = lambda step: lax.dynamic_slice_in_dim(grad_do, (place + step) % ring, 1, 0)[0]
        grad_do = added([at_place(0)] + [around(at_place(step), step) for step in range(1, ring)])
    else:
        grad_do = scatter(grad_do.reshape(-1, hw // chips))
    grad_a = scatter(row_major(grad_a))

    def from_chips(values):
        return [values] + [to_chip(values, step) for step in range(1, chips)]

    def whole_columns(half, other, at, size):
        return in_order(half[:, at : at + size], other[:, at : at + size], 1).astype(f32)

    ff_half = gate_mat.shape[1]
    half = added(from_chips(grad_b))
    other = swap(half)
    share_gate, share_up = (whole_columns(half, other, k * ff_half, ff_half) for k in range(2))
    def chip_order(got):
        return [
            functools.reduce(
                lambda kept, back: jnp.where((chip - back) % chips == which, got[back], kept),
                range(1, chips), got[0],
            )
            for which in range(chips)
        ]

    half = jnp.concatenate(chip_order(from_chips(grad_do)), axis=1)
    both = whole_columns(half, swap(half), 0, hw)
    share_down, share_output = both[: w_down.shape[0]], both[w_down.shape[0] :]
    got, share = from_chips(grad_a), hw // chips
    at_v = 2 * share
    half = jnp.concatenate(
        [
            piece for k in range(2)
            for piece in chip_order([g[:, k * share : (k + 1) * share] for g in got])
        ]
        + [added([g[:, at_v : at_v + hw] for g in got])]
        + [g[:, at_v + hw :] for g in got],
        axis=1,
    )
    other = swap(half)
    share_query, share_key, share_value = (
        whole_columns(half, other, k * hw, hw) for k in range(3)
    )
    gain_sums = sum(
        which[:, at : at + LANES].astype(f32)
        for which in (half, other) for at in range(3 * hw, half.shape[1], LANES)
    )
    share_gain_one, share_gain_two = gain_sums[:, 0], gain_sums[:, 1]
    squares = jnp.sum(gain_sums[:, 2:8], axis=0).reshape(3, 2).sum(axis=0)
    value_norms = jnp.sqrt(squares / f32(dp * fsdp * length * width))
    return (
        block_out, input_grad, share_gain_one, share_query, share_key, share_value, share_output,
        share_gain_two, share_gate, share_up, share_down, v1_grad_out, value_norms,
    )


def solution(mesh):
    tokens = ("dp", "fsdp")
    in_specs = (
        P(tokens, None, None), P(tokens, None, None), P(tokens, None), P("fsdp"),
        P("fsdp", None), P("fsdp", None), P("fsdp", None), P("fsdp", None), P("fsdp"),
        P("fsdp", None), P("fsdp", None), P("fsdp", None), P(tokens, None, None),
        P(tokens, None, None),
    )
    out_specs = (
        P(tokens, None, None), P(tokens, None, None), P("fsdp"), P("fsdp", None),
        P("fsdp", None), P("fsdp", None), P("fsdp", None), P("fsdp"), P("fsdp", None),
        P("fsdp", None), P("fsdp", None), P(tokens, None, None), P(),
    )
    return jax.shard_map(shards, mesh=mesh, in_specs=in_specs, out_specs=out_specs, check_vma=False)
```

```python
import functools
import math

import jax
import jax.numpy as jnp
from jax import lax
from jax.experimental import pallas as pl
from jax.experimental.layout import Layout, with_layout_constraint
from jax.experimental.pallas import tpu as pltpu
from jax.sharding import PartitionSpec as P

HEAD_DIM = 64
LANES = 128
REACH = 256
BLOCK = 128

eps_norm = 1e-06
rope_base = 10000.0
masked_score = -1e30
bf16 = jnp.bfloat16
f32 = jnp.float32


def positions_of(segment_ids):
    places = lax.broadcasted_iota(jnp.int32, segment_ids.shape, 1)
    before = jnp.concatenate([segment_ids[:, :1] - 1, segment_ids[:, :-1]], axis=1)
    starts = jnp.where(segment_ids != before, places, jnp.zeros_like(places))
    return places - lax.cummax(starts, axis=1)


def rope_tables(positions):
    half = HEAD_DIM // 2
    lane = lax.broadcasted_iota(jnp.int32, (1, LANES), 1)
    inverse = jnp.exp((lane % half).astype(f32) * (-math.log(rope_base) / half))
    angles = positions.astype(f32)[:, None] * inverse
    sign = jnp.where(lane % HEAD_DIM < half, -1.0, 1.0).astype(f32)
    return jnp.cos(angles), jnp.sin(angles) * sign


def halves_swapped(u):
    half = HEAD_DIM // 2
    lane = lax.broadcasted_iota(jnp.int32, u.shape, 1)
    return jnp.where(
        lane % HEAD_DIM < half, pltpu.roll(u, LANES - half, 1), pltpu.roll(u, half, 1)
    )


def head_lanes(u, head):
    lane = lax.broadcasted_iota(jnp.int32, u.shape, 1)
    return jnp.where(lane // HEAD_DIM == head, u, jnp.zeros_like(u))


def row_major(values):
    return with_layout_constraint(values, Layout(major_to_minor=(0, 1)))


def dot_nt(a, b):
    return lax.dot_general(a, b, (((1,), (1,)), ((), ())), preferred_element_type=f32)


def dot_tn(a, b):
    return lax.dot_general(a, b, (((0,), (0,)), ((), ())), preferred_element_type=f32)


def dot_nn(a, b):
    return jnp.dot(a, b, preferred_element_type=f32)


def softmax_block(q_head, k_rows, begin, first_key, starts):
    scores = dot_nt(q_head, k_rows) * (HEAD_DIM ** (-0.5))
    row = begin + lax.broadcasted_iota(jnp.int32, scores.shape, 0)
    col = first_key + lax.broadcasted_iota(jnp.int32, scores.shape, 1)
    allowed = (col <= row) & (col >= starts)
    scores = jnp.where(allowed, scores, masked_score)
    expo = jnp.exp(scores - jnp.max(scores, axis=1, keepdims=True))
    return expo / jnp.sum(expo, axis=1, keepdims=True)


def key_range(begin):
    return max(0, (begin - REACH + 1) // BLOCK * BLOCK), begin + BLOCK


def attend_kernel(
    start_ref, cos_ref, sin_ref, q_ref, k_ref, v_ref, first_ref,
    out_ref, q_rot_ref, k_rot_ref, blend_ref,
):
    cosine, sine = cos_ref[...], sin_ref[...]
    queries, keys = q_ref[...], k_ref[...]
    q_rot = (queries * cosine + halves_swapped(queries) * sine).astype(bf16)
    k_rot = (keys * cosine + halves_swapped(keys) * sine).astype(bf16)
    blended = (0.5 * v_ref[...] + 0.5 * first_ref[...].astype(f32)).astype(bf16)
    q_rot_ref[...] = q_rot
    k_rot_ref[...] = k_rot
    blend_ref[...] = blended
    for begin in range(0, q_rot.shape[0], BLOCK):
        low, high = key_range(begin)
        starts = start_ref[begin : begin + BLOCK, :]
        total = jnp.zeros((BLOCK, LANES), f32)
        for head in range(LANES // HEAD_DIM):
            q_head = head_lanes(q_rot[begin : begin + BLOCK, :], head)
            probs = softmax_block(q_head, k_rot[low:high, :], begin, low, starts)
            total = total + dot_nn(probs.astype(bf16), head_lanes(blended[low:high, :], head))
        out_ref[begin : begin + BLOCK, :] = total.astype(bf16)


def attend_back_kernel(
    start_ref, cos_ref, sin_ref, q_rot_ref, k_rot_ref, blend_ref, grad_ref,
    dq_ref, dk_ref, dv_ref, dk_sum, dv_sum,
):
    scale = HEAD_DIM ** (-0.5)
    cosine, sine = cos_ref[...], sin_ref[...]
    q_rot, k_rot, blended, grads = q_rot_ref[...], k_rot_ref[...], blend_ref[...], grad_ref[...]
    dk_sum[...] = jnp.zeros_like(dk_sum)
    dv_sum[...] = jnp.zeros_like(dv_sum)
    for begin in range(0, q_rot.shape[0], BLOCK):
        low, high = key_range(begin)
        rows = slice(begin, begin + BLOCK)
        starts = start_ref[rows, :]
        dq = jnp.zeros((BLOCK, LANES), f32)
        for head in range(LANES // HEAD_DIM):
            q_head = head_lanes(q_rot[rows, :], head)
            k_head = head_lanes(k_rot[low:high, :], head)
            g_head = head_lanes(grads[rows, :], head)
            probs = softmax_block(q_head, k_rot[low:high, :], begin, low, starts)
            grad_probs = dot_nt(g_head, blended[low:high, :])
            inner = jnp.sum(probs * grad_probs, axis=1, keepdims=True)
            grad_scores = (probs * (grad_probs - inner)).astype(bf16)
            dq = dq + dot_nn(grad_scores, k_head)
            dk_sum[low:high, :] += dot_tn(grad_scores, q_head)
            dv_sum[low:high, :] += dot_tn(probs.astype(bf16), g_head)
        dq = dq * scale
        dq_ref[rows, :] = (
            dq * cosine[rows, :] - halves_swapped(dq) * sine[rows, :]
        ).astype(bf16)
    dk = dk_sum[...] * scale
    dk_ref[...] = (dk * cosine - halves_swapped(dk) * sine).astype(bf16)
    dv_ref[...] = (0.5 * dv_sum[...]).astype(bf16)


def attend(starts, cosine, sine, qkv, first, length):
    tokens, width = first.shape
    pairs = width // LANES
    per_row = lambda lanes: pl.BlockSpec((length, lanes), lambda r, h: (r, 0))
    part = lambda k: pl.BlockSpec((length, LANES), lambda r, h: (r, k * pairs + h))
    return pl.pallas_call(
        attend_kernel,
        grid=(tokens // length, pairs),
        in_specs=[per_row(1), per_row(LANES), per_row(LANES), part(0), part(1), part(2), part(0)],
        out_specs=[part(0)] * 4,
        out_shape=[jax.ShapeDtypeStruct((tokens, width), bf16)] * 4,
        name="attend",
    )(starts, cosine, sine, qkv, qkv, qkv, first)


def attend_back(starts, cosine, sine, q_rot, k_rot, blended, grads, length):
    tokens, width = grads.shape
    per_row = lambda lanes: pl.BlockSpec((length, lanes), lambda r, h: (r, 0))
    part = pl.BlockSpec((length, LANES), lambda r, h: (r, h))
    return pl.pallas_call(
        attend_back_kernel,
        grid=(tokens // length, width // LANES),
        in_specs=[per_row(1), per_row(LANES), per_row(LANES)] + [part] * 4,
        out_specs=[part] * 3,
        out_shape=[jax.ShapeDtypeStruct((tokens, width), bf16)] * 3,
        scratch_shapes=[pltpu.VMEM((length, LANES), f32)] * 2,
        name="attend_back",
    )(starts, cosine, sine, q_rot, k_rot, blended, grads)


def order_kernel(at_ref, *refs):
    *pieces, out_ref = refs
    count = len(pieces)
    for step, piece in enumerate(pieces):
        out_ref[lax.rem(at_ref[0] + count - step, count)] = piece[...]


def in_ring_order(place, pieces):
    in_vmem = pl.BlockSpec(memory_space=pltpu.VMEM)
    return pl.pallas_call(
        order_kernel,
        in_specs=[pl.BlockSpec(memory_space=pltpu.SMEM)] + [in_vmem] * len(pieces),
        out_specs=in_vmem,
        out_shape=jax.ShapeDtypeStruct((len(pieces),) + pieces[0].shape, pieces[0].dtype),
        name="ring_order",
    )(jnp.stack([place]), *pieces)


def join_kernel(at_ref, mine_ref, far_ref, other_ref, out_ref):
    size = other_ref.shape[3]
    shared = mine_ref.shape[2] - size
    side, chip = at_ref[0], at_ref[1]
    for from_side, own in enumerate((mine_ref, far_ref)):
        row = side if from_side == 0 else 1 - side
        if shared:
            out_ref[:, row, :, :shared] = own[:, :, :shared]
        for which in range(2):
            @pl.when(chip == which)
            def _():
                first, second = shared + which * size, shared + (1 - which) * size
                out_ref[:, row, :, first : first + size] = own[:, :, shared:]
                out_ref[:, row, :, second : second + size] = other_ref[from_side]


def joined(side, chip, mine, far, other):
    ring, height, held = mine.shape
    in_vmem = pl.BlockSpec(memory_space=pltpu.VMEM)
    full = jax.ShapeDtypeStruct((ring, 2, height, held + other.shape[3]), mine.dtype)
    whole = pl.pallas_call(
        join_kernel,
        in_specs=[pl.BlockSpec(memory_space=pltpu.SMEM)] + [in_vmem] * 3,
        out_specs=in_vmem,
        out_shape=full,
        name="joined",
    )(jnp.stack([side, chip]), mine, far, other)
    return whole.reshape(ring * 2 * height, full.shape[3])


def norm_stats(values):
    return lax.rsqrt(jnp.mean(values * values, axis=-1, keepdims=True) + eps_norm)


def norm_backward(values, inverse, gain_f, grad_out):
    scaled = values * inverse
    grad_scaled = grad_out * gain_f
    grad_gain = jnp.sum(grad_out * scaled, axis=0)
    grad_values = inverse * (
        grad_scaled - scaled * jnp.mean(grad_scaled * scaled, axis=-1, keepdims=True)
    )
    return grad_values, grad_gain


def shards(
    hidden_in, value_first, segment_ids, attn_gain, w_query, w_key, w_value, w_output,
    mlp_gain, w_gate, w_up, w_down, out_grad, v1_grad_acc,
):
    length, width = hidden_in.shape[1:]
    dp, fsdp = lax.axis_size("dp"), lax.axis_size("fsdp")
    core, chip = lax.axis_index("dp") % 2, lax.axis_index("dp") // 2
    chips = dp // 2
    hw = width // 2

    def swap(values):
        return lax.ppermute(values, "dp", [(i, i ^ 1) for i in range(dp)])

    def to_chip(values, step):
        return lax.ppermute(values, "dp", [(i, (i + 2 * step) % dp) for i in range(dp)])

    def part(values, which):
        share = values.shape[-1] // chips
        return lax.dynamic_slice_in_dim(values, which * share, share, values.ndim - 1)

    def chip_parts(values):
        return [part(values, chip)] + [
            to_chip(part(values, (chip + step) % chips), step) for step in range(1, chips)
        ]

    def added(parts):
        return sum(p.astype(f32) for p in parts).astype(bf16)

    def pair(values):
        return jnp.concatenate([values, swap(values)], axis=0)

    def cols(values, which):
        half = values.shape[-1] // 2
        return lax.dynamic_slice_in_dim(values, which * half, half, values.ndim - 1)

    def rows(values, which):
        half = values.shape[0] // 2
        return lax.dynamic_slice_in_dim(values, which * half, half, 0)

    def in_order(mine, other, axis):
        return jnp.concatenate(
            [jnp.where(core == 0, mine, other), jnp.where(core == 0, other, mine)], axis=axis
        )

    def rows_from_cols(mine):
        return in_order(rows(mine, core), swap(rows(mine, 1 - core)), 1)

    def cols_from_rows(mine):
        return in_order(cols(mine, core), swap(cols(mine, 1 - core)), 0)

    def gather(shard):
        return lax.all_gather(shard, "fsdp", axis=0, tiled=True)

    def scatter(whole):
        return lax.psum_scatter(whole, "fsdp", scatter_dimension=0, tiled=True)

    ring, place = fsdp // 2, lax.axis_index("fsdp") // 2
    side = lax.axis_index("fsdp") % 2

    def sides(values):
        return lax.ppermute(values, "fsdp", [(i, i ^ 1) for i in range(fsdp)])

    def around(values, step):
        return lax.ppermute(values, "fsdp", [(i, (i + 2 * step) % fsdp) for i in range(fsdp)])

    def shared_lanes(shard):
        lanes = shard.shape[1] // LANES
        return (lanes - 2 * (lanes // 2)) * LANES

    def held_columns(shard):
        shared = shared_lanes(shard)
        size = (shard.shape[1] - shared) // 2
        held = lax.dynamic_slice_in_dim(shard, shared + chip * size, size, 1)
        return jnp.concatenate([shard[:, :shared], held], axis=1) if shared else held

    def ring_pieces(held):
        return [held] + [around(held, step) for step in range(1, ring)]

    def swapped_halves(shard, mine, far):
        shared = shared_lanes(shard)
        return jnp.stack([mine[:, :, shared:], far[:, :, shared:]])

    def mine_and_partner(partial):
        return partial[:length] + swap(partial[length:].astype(bf16)).astype(f32)

    gains = jnp.stack([attn_gain, mlp_gain])
    gains = jnp.pad(gains, ((0, w_query.shape[0] - 2), (0, max(0, LANES - gains.shape[1]))))
    by_ring, tie = chips == 2 and fsdp <= 8, lax.optimization_barrier
    shard_a = jnp.concatenate([gains] + [cols(w, core) for w in (w_query, w_key, w_value)], axis=1)
    shard_b = jnp.concatenate([cols(w_output, core), cols(w_gate, core)], axis=1)
    height, down_height = w_query.shape[0], w_down.shape[0]
    blocks = -(-down_height // height)
    shard_d = jnp.pad(cols(w_down, core), ((0, blocks * height - down_height), (0, 0)))
    shard_c = jnp.concatenate(
        [cols(w_up, core)] + [shard_d[k * height : (k + 1) * height] for k in range(blocks)], axis=1
    )
    if by_ring:
        join = functools.partial(joined, side, chip)
        pieces_a = ring_pieces(held_columns(shard_a))
        pieces_a, held_b = tie((pieces_a, held_columns(shard_b)))
        pieces_b = ring_pieces(held_b)
        mine_a = in_ring_order(place, pieces_a)
        far_a = sides(mine_a)
        pieces_b, far_a, mine_a, shard_c = tie((pieces_b, far_a, mine_a, shard_c))
        mine_b = in_ring_order(place, pieces_b)
        halves_a = swapped_halves(shard_a, mine_a, far_a)
        mine_b, halves_a = tie((mine_b, halves_a))
        far_b, other_a = sides(mine_b), to_chip(halves_a, 1)
        far_b, other_a = tie((far_b, other_a))
        halves_b = swapped_halves(shard_b, mine_b, far_b)
        halves_b, other_a = tie((halves_b, other_a))
        other_b = to_chip(halves_b, 1)
        whole_a = join(mine_a, far_a, other_a)
    else:
        whole_a = gather(shard_a)
    whole_c = gather(shard_c)
    up_mat, whole_d = whole_c[:, : w_up.shape[1] // 2], whole_c[:, w_up.shape[1] // 2 :]
    qkv_mat = whole_a[:, gains.shape[1] :]
    gain_rows = whole_a[:, : gains.shape[1]].reshape(fsdp, w_query.shape[0], -1)
    gain_one = gain_rows[:, 0, : attn_gain.shape[0]].reshape(1, width).astype(f32)
    gain_two = gain_rows[:, 1, : attn_gain.shape[0]].reshape(1, width).astype(f32)

    segments = pair(segment_ids)
    positions = positions_of(segments)
    starts = (lax.broadcasted_iota(jnp.int32, positions.shape, 1) - positions).reshape(-1, 1)
    cosine, sine = rope_tables(positions.reshape(-1))
    hidden = pair(hidden_in[0]).astype(f32)
    first = value_first[0]
    first_half = jnp.concatenate([cols(first, core), swap(cols(first, 1 - core))], axis=0)
    cotangent = pair(out_grad[0])

    inverse_one = norm_stats(hidden)
    normed = (hidden * inverse_one * gain_one).astype(bf16)
    qkv = dot_nn(normed, qkv_mat)
    attended, q_rot, k_rot, blended = attend(starts, cosine, sine, qkv, first_half, length)
    if by_ring:
        attended, other_b = tie((attended, other_b))
        whole_b = join(mine_b, far_b, other_b)
    else:
        whole_b = gather(shard_b)
    output_mat, gate_mat = rows_from_cols(whole_b[:, :hw]), whole_b[:, hw:]
    first_f, blended_f = first.astype(f32), blended.astype(f32)
    square_first, square_blend = jnp.sum(first_f * first_f), jnp.sum(blended_f * blended_f)

    mixed = hidden[:length] + mine_and_partner(dot_nn(attended, output_mat))
    inverse_two = norm_stats(mixed)
    normed_two = pair((mixed * inverse_two * gain_two).astype(bf16))
    gate = dot_nn(normed_two, gate_mat)
    up_val = dot_nn(normed_two, up_mat)

    def unpacked(packed):
        stacked = jnp.concatenate(
            [packed[:, k * hw : (k + 1) * hw].reshape(-1, height, hw) for k in range(blocks)], axis=1
        )
        return stacked[:, :down_height].reshape(-1, hw)

    down_mat = in_order(unpacked(rows(whole_d, core)), unpacked(swap(rows(whole_d, 1 - core))), 1)
    sigma = jax.nn.sigmoid(gate)
    silu_gate = gate * sigma
    act = (silu_gate * up_val).astype(bf16)
    block_out = (mixed + mine_and_partner(dot_nn(act, down_mat))).astype(bf16)[None]

    grad_act = dot_nt(cotangent, down_mat)
    grad_gate = (grad_act * up_val * sigma * (1.0 + gate * (1.0 - sigma))).astype(bf16)
    grad_upv = (grad_act * silu_gate).astype(bf16)
    grad_b = jnp.concatenate(
        [dot_tn(normed_two, grad_gate).astype(bf16), dot_tn(normed_two, grad_upv).astype(bf16)],
        axis=1,
    )
    grad_b, act, grad_gate, grad_upv = tie((grad_b, act, grad_gate, grad_upv))
    grad_b = scatter(grad_b)
    grad_down = chip_parts(cols_from_rows(dot_tn(act, cotangent).astype(bf16)))
    grad_normed_two = mine_and_partner(
        dot_nt(grad_gate, gate_mat) + dot_nt(grad_upv, up_mat)
    )
    grad_mixed_norm, grad_gain_two = norm_backward(mixed, inverse_two, gain_two, grad_normed_two)
    grad_mixed = out_grad[0].astype(f32) + grad_mixed_norm
    grad_attn = pair(grad_mixed.astype(bf16))
    grad_out_w = cols_from_rows(dot_tn(attended, grad_attn).astype(bf16))
    grad_attended = dot_nt(grad_attn, output_mat).astype(bf16)
    grad_out_w = chip_parts(grad_out_w)
    dq, dk, dv = attend_back(starts, cosine, sine, q_rot, k_rot, blended, grad_attended, length)
    grad_normed = mine_and_partner(
        dot_nt(dq, qkv_mat[:, :hw]) + dot_nt(dk, qkv_mat[:, hw : 2 * hw])
        + dot_nt(dv, qkv_mat[:, 2 * hw :])
    )
    grad_rows_norm, grad_gain_one = norm_backward(
        hidden[:length], inverse_one[:length], gain_one, grad_normed
    )
    input_grad = (grad_mixed + grad_rows_norm)[None]
    grad_first = in_order(dv[:length], swap(dv[length:]), 1)
    v1_grad_out = v1_grad_acc + grad_first.astype(f32)[None]

    rest = jnp.stack([square_first, square_blend])
    terms = []
    for _ in range(3):
        terms.append(lax.reduce_precision(rest, 8, 7))
        rest = rest - terms[-1]
    terms = jnp.concatenate([jnp.zeros((2,), f32)] + terms)
    row = lax.broadcasted_iota(jnp.int32, (width, 1), 0) % attn_gain.shape[0]
    extra = jnp.concatenate(
        [
            grad_gain_one[:, None], grad_gain_two[:, None],
            jnp.where(row == lax.axis_index("fsdp"), terms[None, 2:], 0.0),
        ],
        axis=1,
    )
    extra = jnp.pad(extra, ((0, 0), (0, LANES - extra.shape[1]))).astype(bf16)
    grad_q, grad_k = (chip_parts(dot_tn(normed, d).astype(bf16)) for d in (dq, dk))
    grad_v = dot_tn(normed, dv).astype(bf16)
    grad_a = jnp.concatenate([added(grad_q), added(grad_k), grad_v, extra], axis=1)
    grad_a, grad_b, grad_down, grad_out_w = tie((grad_a, grad_b, grad_down, grad_out_w))
    grad_do = jnp.concatenate(
        [added(parts).reshape(fsdp, -1, hw // chips) for parts in (grad_down, grad_out_w)], axis=1
    )
    if by_ring:
        grad_do = grad_do.reshape(ring, 2, *grad_do.shape[1:])
        at_side = lambda which: lax.dynamic_slice_in_dim(grad_do, which, 1, 1)[:, 0]
        grad_do = added([at_side(side), sides(at_side(1 - side))])
        at_place = lambda step: lax.dynamic_slice_in_dim(grad_do, (place + step) % ring, 1, 0)[0]
        grad_do = added([at_place(0)] + [around(at_place(step), step) for step in range(1, ring)])
    else:
        grad_do = scatter(grad_do.reshape(-1, hw // chips))
    grad_a = scatter(row_major(grad_a))

    def from_chips(values):
        return [values] + [to_chip(values, step) for step in range(1, chips)]

    def whole_columns(half, other, at, size):
        return in_order(half[:, at : at + size], other[:, at : at + size], 1).astype(f32)

    ff_half = gate_mat.shape[1]
    half = added(from_chips(grad_b))
    other = swap(half)
    share_gate, share_up = (whole_columns(half, other, k * ff_half, ff_half) for k in range(2))
    def chip_order(got):
        return [
            functools.reduce(
                lambda kept, back: jnp.where((chip - back) % chips == which, got[back], kept),
                range(1, chips), got[0],
            )
            for which in range(chips)
        ]

    half = jnp.concatenate(chip_order(from_chips(grad_do)), axis=1)
    both = whole_columns(half, swap(half), 0, hw)
    share_down, share_output = both[: w_down.shape[0]], both[w_down.shape[0] :]
    got, share = from_chips(grad_a), hw // chips
    at_v = 2 * share
    half = jnp.concatenate(
        [
            piece for k in range(2)
            for piece in chip_order([g[:, k * share : (k + 1) * share] for g in got])
        ]
        + [added([g[:, at_v : at_v + hw] for g in got])]
        + [g[:, at_v + hw :] for g in got],
        axis=1,
    )
    other = swap(half)
    share_query, share_key, share_value = (
        whole_columns(half, other, k * hw, hw) for k in range(3)
    )
    gain_sums = sum(
        which[:, at : at + LANES].astype(f32)
        for which in (half, other) for at in range(3 * hw, half.shape[1], LANES)
    )
    share_gain_one, share_gain_two = gain_sums[:, 0], gain_sums[:, 1]
    squares = jnp.sum(gain_sums[:, 2:8], axis=0).reshape(3, 2).sum(axis=0)
    value_norms = jnp.sqrt(squares / f32(dp * fsdp * length * width))
    return (
        block_out, input_grad, share_gain_one, share_query, share_key, share_value, share_output,
        share_gain_two, share_gate, share_up, share_down, v1_grad_out, value_norms,
    )


def solution(mesh):
    tokens = ("dp", "fsdp")
    in_specs = (
        P(tokens, None, None), P(tokens, None, None), P(tokens, None), P("fsdp"),
        P("fsdp", None), P("fsdp", None), P("fsdp", None), P("fsdp", None), P("fsdp"),
        P("fsdp", None), P("fsdp", None), P("fsdp", None), P(tokens, None, None),
        P(tokens, None, None),
    )
    out_specs = (
        P(tokens, None, None), P(tokens, None, None), P("fsdp"), P("fsdp", None),
        P("fsdp", None), P("fsdp", None), P("fsdp", None), P("fsdp"), P("fsdp", None),
        P("fsdp", None), P("fsdp", None), P(tokens, None, None), P(),
    )
    return jax.shard_map(shards, mesh=mesh, in_specs=in_specs, out_specs=out_specs, check_vma=False)
```

```python
import functools
import math

import jax
import jax.numpy as jnp
from jax import lax
from jax.experimental import pallas as pl
from jax.experimental.layout import Layout, with_layout_constraint
from jax.experimental.pallas import tpu as pltpu
from jax.sharding import PartitionSpec as P

HEAD_DIM = 64
LANES = 128
REACH = 256
BLOCK = 128

eps_norm = 1e-06
rope_base = 10000.0
masked_score = -1e30
bf16 = jnp.bfloat16
f32 = jnp.float32


def positions_of(segment_ids):
    places = lax.broadcasted_iota(jnp.int32, segment_ids.shape, 1)
    before = jnp.concatenate([segment_ids[:, :1] - 1, segment_ids[:, :-1]], axis=1)
    starts = jnp.where(segment_ids != before, places, jnp.zeros_like(places))
    return places - lax.cummax(starts, axis=1)


def rope_tables(positions):
    half = HEAD_DIM // 2
    lane = lax.broadcasted_iota(jnp.int32, (1, LANES), 1)
    inverse = jnp.exp((lane % half).astype(f32) * (-math.log(rope_base) / half))
    angles = positions.astype(f32)[:, None] * inverse
    sign = jnp.where(lane % HEAD_DIM < half, -1.0, 1.0).astype(f32)
    return jnp.cos(angles), jnp.sin(angles) * sign


def halves_swapped(u):
    half = HEAD_DIM // 2
    lane = lax.broadcasted_iota(jnp.int32, u.shape, 1)
    return jnp.where(
        lane % HEAD_DIM < half, pltpu.roll(u, LANES - half, 1), pltpu.roll(u, half, 1)
    )


def head_lanes(u, head):
    lane = lax.broadcasted_iota(jnp.int32, u.shape, 1)
    return jnp.where(lane // HEAD_DIM == head, u, jnp.zeros_like(u))


def row_major(values):
    return with_layout_constraint(values, Layout(major_to_minor=(0, 1)))


def dot_nt(a, b):
    return lax.dot_general(a, b, (((1,), (1,)), ((), ())), preferred_element_type=f32)


def dot_tn(a, b):
    return lax.dot_general(a, b, (((0,), (0,)), ((), ())), preferred_element_type=f32)


def dot_nn(a, b):
    return jnp.dot(a, b, preferred_element_type=f32)


def softmax_block(q_head, k_rows, begin, first_key, starts):
    scores = dot_nt(q_head, k_rows) * (HEAD_DIM ** (-0.5))
    row = begin + lax.broadcasted_iota(jnp.int32, scores.shape, 0)
    col = first_key + lax.broadcasted_iota(jnp.int32, scores.shape, 1)
    allowed = (col <= row) & (col >= starts)
    scores = jnp.where(allowed, scores, masked_score)
    expo = jnp.exp(scores - jnp.max(scores, axis=1, keepdims=True))
    return expo / jnp.sum(expo, axis=1, keepdims=True)


def key_range(begin):
    return max(0, (begin - REACH + 1) // BLOCK * BLOCK), begin + BLOCK


def attend_kernel(
    start_ref, cos_ref, sin_ref, q_ref, k_ref, v_ref, first_ref,
    out_ref, q_rot_ref, k_rot_ref, blend_ref,
):
    cosine, sine = cos_ref[...], sin_ref[...]
    queries, keys = q_ref[...], k_ref[...]
    q_rot = (queries * cosine + halves_swapped(queries) * sine).astype(bf16)
    k_rot = (keys * cosine + halves_swapped(keys) * sine).astype(bf16)
    blended = (0.5 * v_ref[...] + 0.5 * first_ref[...].astype(f32)).astype(bf16)
    q_rot_ref[...] = q_rot
    k_rot_ref[...] = k_rot
    blend_ref[...] = blended
    for begin in range(0, q_rot.shape[0], BLOCK):
        low, high = key_range(begin)
        starts = start_ref[begin : begin + BLOCK, :]
        total = jnp.zeros((BLOCK, LANES), f32)
        for head in range(LANES // HEAD_DIM):
            q_head = head_lanes(q_rot[begin : begin + BLOCK, :], head)
            probs = softmax_block(q_head, k_rot[low:high, :], begin, low, starts)
            total = total + dot_nn(probs.astype(bf16), head_lanes(blended[low:high, :], head))
        out_ref[begin : begin + BLOCK, :] = total.astype(bf16)


def attend_back_kernel(
    start_ref, cos_ref, sin_ref, q_rot_ref, k_rot_ref, blend_ref, grad_ref,
    dq_ref, dk_ref, dv_ref, dk_sum, dv_sum,
):
    scale = HEAD_DIM ** (-0.5)
    cosine, sine = cos_ref[...], sin_ref[...]
    q_rot, k_rot, blended, grads = q_rot_ref[...], k_rot_ref[...], blend_ref[...], grad_ref[...]
    dk_sum[...] = jnp.zeros_like(dk_sum)
    dv_sum[...] = jnp.zeros_like(dv_sum)
    for begin in range(0, q_rot.shape[0], BLOCK):
        low, high = key_range(begin)
        rows = slice(begin, begin + BLOCK)
        starts = start_ref[rows, :]
        dq = jnp.zeros((BLOCK, LANES), f32)
        for head in range(LANES // HEAD_DIM):
            q_head = head_lanes(q_rot[rows, :], head)
            k_head = head_lanes(k_rot[low:high, :], head)
            g_head = head_lanes(grads[rows, :], head)
            probs = softmax_block(q_head, k_rot[low:high, :], begin, low, starts)
            grad_probs = dot_nt(g_head, blended[low:high, :])
            inner = jnp.sum(probs * grad_probs, axis=1, keepdims=True)
            grad_scores = (probs * (grad_probs - inner)).astype(bf16)
            dq = dq + dot_nn(grad_scores, k_head)
            dk_sum[low:high, :] += dot_tn(grad_scores, q_head)
            dv_sum[low:high, :] += dot_tn(probs.astype(bf16), g_head)
        dq = dq * scale
        dq_ref[rows, :] = (
            dq * cosine[rows, :] - halves_swapped(dq) * sine[rows, :]
        ).astype(bf16)
    dk = dk_sum[...] * scale
    dk_ref[...] = (dk * cosine - halves_swapped(dk) * sine).astype(bf16)
    dv_ref[...] = (0.5 * dv_sum[...]).astype(bf16)


def attend(starts, cosine, sine, qkv, first, length):
    tokens, width = first.shape
    pairs = width // LANES
    per_row = lambda lanes: pl.BlockSpec((length, lanes), lambda r, h: (r, 0))
    part = lambda k: pl.BlockSpec((length, LANES), lambda r, h: (r, k * pairs + h))
    return pl.pallas_call(
        attend_kernel,
        grid=(tokens // length, pairs),
        in_specs=[per_row(1), per_row(LANES), per_row(LANES), part(0), part(1), part(2), part(0)],
        out_specs=[part(0)] * 4,
        out_shape=[jax.ShapeDtypeStruct((tokens, width), bf16)] * 4,
        name="attend",
    )(starts, cosine, sine, qkv, qkv, qkv, first)


def attend_back(starts, cosine, sine, q_rot, k_rot, blended, grads, length):
    tokens, width = grads.shape
    per_row = lambda lanes: pl.BlockSpec((length, lanes), lambda r, h: (r, 0))
    part = pl.BlockSpec((length, LANES), lambda r, h: (r, h))
    return pl.pallas_call(
        attend_back_kernel,
        grid=(tokens // length, width // LANES),
        in_specs=[per_row(1), per_row(LANES), per_row(LANES)] + [part] * 4,
        out_specs=[part] * 3,
        out_shape=[jax.ShapeDtypeStruct((tokens, width), bf16)] * 3,
        scratch_shapes=[pltpu.VMEM((length, LANES), f32)] * 2,
        name="attend_back",
    )(starts, cosine, sine, q_rot, k_rot, blended, grads)


def order_kernel(at_ref, *refs):
    *pieces, out_ref = refs
    count = len(pieces)
    for step, piece in enumerate(pieces):
        out_ref[lax.rem(at_ref[0] + count - step, count)] = piece[...]


def in_ring_order(place, pieces):
    in_vmem = pl.BlockSpec(memory_space=pltpu.VMEM)
    return pl.pallas_call(
        order_kernel,
        in_specs=[pl.BlockSpec(memory_space=pltpu.SMEM)] + [in_vmem] * len(pieces),
        out_specs=in_vmem,
        out_shape=jax.ShapeDtypeStruct((len(pieces),) + pieces[0].shape, pieces[0].dtype),
        name="ring_order",
    )(jnp.stack([place]), *pieces)


def join_kernel(at_ref, mine_ref, far_ref, mine_other_ref, far_other_ref, out_ref):
    size = mine_other_ref.shape[2]
    shared = mine_ref.shape[2] - size
    side, chip = at_ref[0], at_ref[1]
    for own, other_ref, row in (
        (mine_ref, mine_other_ref, side), (far_ref, far_other_ref, 1 - side)
    ):
        if shared:
            out_ref[:, row, :, :shared] = own[:, :, :shared]
        for which in range(2):
            @pl.when(chip == which)
            def _():
                first, second = shared + which * size, shared + (1 - which) * size
                out_ref[:, row, :, first : first + size] = own[:, :, shared:]
                out_ref[:, row, :, second : second + size] = other_ref[...]


def joined(side, chip, mine, far, mine_other, far_other):
    ring, height, held = mine.shape
    in_vmem = pl.BlockSpec(memory_space=pltpu.VMEM)
    full = jax.ShapeDtypeStruct((ring, 2, height, held + mine_other.shape[2]), mine.dtype)
    whole = pl.pallas_call(
        join_kernel,
        in_specs=[pl.BlockSpec(memory_space=pltpu.SMEM)] + [in_vmem] * 4,
        out_specs=in_vmem,
        out_shape=full,
        name="joined",
    )(jnp.stack([side, chip]), mine, far, mine_other, far_other)
    return whole.reshape(ring * 2 * height, full.shape[3])


def norm_stats(values):
    return lax.rsqrt(jnp.mean(values * values, axis=-1, keepdims=True) + eps_norm)


def norm_backward(values, inverse, gain_f, grad_out):
    scaled = values * inverse
    grad_scaled = grad_out * gain_f
    grad_gain = jnp.sum(grad_out * scaled, axis=0)
    grad_values = inverse * (
        grad_scaled - scaled * jnp.mean(grad_scaled * scaled, axis=-1, keepdims=True)
    )
    return grad_values, grad_gain


def shards(
    hidden_in, value_first, segment_ids, attn_gain, w_query, w_key, w_value, w_output,
    mlp_gain, w_gate, w_up, w_down, out_grad, v1_grad_acc,
):
    length, width = hidden_in.shape[1:]
    dp, fsdp = lax.axis_size("dp"), lax.axis_size("fsdp")
    core, chip = lax.axis_index("dp") % 2, lax.axis_index("dp") // 2
    chips = dp // 2
    hw = width // 2

    def swap(values):
        return lax.ppermute(values, "dp", [(i, i ^ 1) for i in range(dp)])

    def to_chip(values, step):
        return lax.ppermute(values, "dp", [(i, (i + 2 * step) % dp) for i in range(dp)])

    def part(values, which):
        share = values.shape[-1] // chips
        return lax.dynamic_slice_in_dim(values, which * share, share, values.ndim - 1)

    def chip_parts(values):
        return [part(values, chip)] + [
            to_chip(part(values, (chip + step) % chips), step) for step in range(1, chips)
        ]

    def added(parts):
        return sum(p.astype(f32) for p in parts).astype(bf16)

    def pair(values):
        return jnp.concatenate([values, swap(values)], axis=0)

    def cols(values, which):
        half = values.shape[-1] // 2
        return lax.dynamic_slice_in_dim(values, which * half, half, values.ndim - 1)

    def rows(values, which):
        half = values.shape[0] // 2
        return lax.dynamic_slice_in_dim(values, which * half, half, 0)

    def in_order(mine, other, axis):
        return jnp.concatenate(
            [jnp.where(core == 0, mine, other), jnp.where(core == 0, other, mine)], axis=axis
        )

    def rows_from_cols(mine):
        return in_order(rows(mine, core), swap(rows(mine, 1 - core)), 1)

    def cols_from_rows(mine):
        return in_order(cols(mine, core), swap(cols(mine, 1 - core)), 0)

    def gather(shard):
        return lax.all_gather(shard, "fsdp", axis=0, tiled=True)

    def scatter(whole):
        return lax.psum_scatter(whole, "fsdp", scatter_dimension=0, tiled=True)

    ring, place = fsdp // 2, lax.axis_index("fsdp") // 2
    side = lax.axis_index("fsdp") % 2

    def sides(values):
        return lax.ppermute(values, "fsdp", [(i, i ^ 1) for i in range(fsdp)])

    def around(values, step):
        return lax.ppermute(values, "fsdp", [(i, (i + 2 * step) % fsdp) for i in range(fsdp)])

    def shared_lanes(shard):
        lanes = shard.shape[1] // LANES
        return (lanes - 2 * (lanes // 2)) * LANES

    def held_columns(shard):
        shared = shared_lanes(shard)
        size = (shard.shape[1] - shared) // 2
        held = lax.dynamic_slice_in_dim(shard, shared + chip * size, size, 1)
        return jnp.concatenate([shard[:, :shared], held], axis=1) if shared else held

    def ring_pieces(held):
        return [held] + [around(held, step) for step in range(1, ring)]

    def half_of(shard, values):
        return values[:, :, shared_lanes(shard) :]

    def mine_and_partner(partial):
        return partial[:length] + swap(partial[length:].astype(bf16)).astype(f32)

    gains = jnp.stack([attn_gain, mlp_gain])
    gains = jnp.pad(gains, ((0, w_query.shape[0] - 2), (0, max(0, LANES - gains.shape[1]))))
    by_ring, tie = chips == 2 and fsdp <= 8, lax.optimization_barrier
    shard_a = jnp.concatenate([gains] + [cols(w, core) for w in (w_query, w_key, w_value)], axis=1)
    shard_b = jnp.concatenate([cols(w_output, core), cols(w_gate, core)], axis=1)
    height, down_height = w_query.shape[0], w_down.shape[0]
    blocks = -(-down_height // height)
    shard_d = jnp.pad(cols(w_down, core), ((0, blocks * height - down_height), (0, 0)))
    shard_c = jnp.concatenate(
        [cols(w_up, core)] + [shard_d[k * height : (k + 1) * height] for k in range(blocks)], axis=1
    )
    if by_ring:
        join = functools.partial(joined, side, chip)
        pieces_a = ring_pieces(held_columns(shard_a))
        pieces_a, held_b = tie((pieces_a, held_columns(shard_b)))
        pieces_b = ring_pieces(held_b)
        mine_a = in_ring_order(place, pieces_a)
        mine_a, half_a = tie((mine_a, half_of(shard_a, mine_a)))
        far_a, mine_other_a = sides(mine_a), to_chip(half_a, 1)
        pieces_b, far_a, mine_a, mine_other_a, shard_c = tie(
            (pieces_b, far_a, mine_a, mine_other_a, shard_c)
        )
        half_a = half_of(shard_a, far_a)
        mine_b = in_ring_order(place, pieces_b)
        half_a, mine_b, half_b = tie((half_a, mine_b, half_of(shard_b, mine_b)))
        far_other_a, far_b, mine_other_b = to_chip(half_a, 1), sides(mine_b), to_chip(half_b, 1)
        whole_a = join(mine_a, far_a, mine_other_a, far_other_a)
    else:
        whole_a = gather(shard_a)
    whole_c = gather(shard_c)
    up_mat, whole_d = whole_c[:, : w_up.shape[1] // 2], whole_c[:, w_up.shape[1] // 2 :]
    qkv_mat = whole_a[:, gains.shape[1] :]
    gain_rows = whole_a[:, : gains.shape[1]].reshape(fsdp, w_query.shape[0], -1)
    gain_one = gain_rows[:, 0, : attn_gain.shape[0]].reshape(1, width).astype(f32)
    gain_two = gain_rows[:, 1, : attn_gain.shape[0]].reshape(1, width).astype(f32)

    segments = pair(segment_ids)
    positions = positions_of(segments)
    starts = (lax.broadcasted_iota(jnp.int32, positions.shape, 1) - positions).reshape(-1, 1)
    cosine, sine = rope_tables(positions.reshape(-1))
    hidden = pair(hidden_in[0]).astype(f32)
    first = value_first[0]
    first_half = jnp.concatenate([cols(first, core), swap(cols(first, 1 - core))], axis=0)
    cotangent = pair(out_grad[0])

    inverse_one = norm_stats(hidden)
    normed = (hidden * inverse_one * gain_one).astype(bf16)
    qkv = dot_nn(normed, qkv_mat)
    if by_ring:
        far_b, qkv = tie((far_b, qkv))
        half_b, qkv = tie((half_of(shard_b, far_b), qkv))
        far_other_b = to_chip(half_b, 1)
    attended, q_rot, k_rot, blended = attend(starts, cosine, sine, qkv, first_half, length)
    if by_ring:
        attended, far_b, mine_other_b, far_other_b = tie(
            (attended, far_b, mine_other_b, far_other_b)
        )
        whole_b = join(mine_b, far_b, mine_other_b, far_other_b)
    else:
        whole_b = gather(shard_b)
    output_mat, gate_mat = rows_from_cols(whole_b[:, :hw]), whole_b[:, hw:]
    first_f, blended_f = first.astype(f32), blended.astype(f32)
    square_first, square_blend = jnp.sum(first_f * first_f), jnp.sum(blended_f * blended_f)

    mixed = hidden[:length] + mine_and_partner(dot_nn(attended, output_mat))
    inverse_two = norm_stats(mixed)
    normed_two = pair((mixed * inverse_two * gain_two).astype(bf16))
    gate = dot_nn(normed_two, gate_mat)
    up_val = dot_nn(normed_two, up_mat)

    def unpacked(packed):
        stacked = jnp.concatenate(
            [packed[:, k * hw : (k + 1) * hw].reshape(-1, height, hw) for k in range(blocks)], axis=1
        )
        return stacked[:, :down_height].reshape(-1, hw)

    down_mat = in_order(unpacked(rows(whole_d, core)), unpacked(swap(rows(whole_d, 1 - core))), 1)
    sigma = jax.nn.sigmoid(gate)
    silu_gate = gate * sigma
    act = (silu_gate * up_val).astype(bf16)
    block_out = (mixed + mine_and_partner(dot_nn(act, down_mat))).astype(bf16)[None]

    grad_act = dot_nt(cotangent, down_mat)
    grad_gate = (grad_act * up_val * sigma * (1.0 + gate * (1.0 - sigma))).astype(bf16)
    grad_upv = (grad_act * silu_gate).astype(bf16)
    grad_b = jnp.concatenate(
        [dot_tn(normed_two, grad_gate).astype(bf16), dot_tn(normed_two, grad_upv).astype(bf16)],
        axis=1,
    )
    grad_b, act, grad_gate, grad_upv = tie((grad_b, act, grad_gate, grad_upv))
    grad_b = scatter(grad_b)
    grad_down = chip_parts(cols_from_rows(dot_tn(act, cotangent).astype(bf16)))
    grad_normed_two = mine_and_partner(
        dot_nt(grad_gate, gate_mat) + dot_nt(grad_upv, up_mat)
    )
    grad_mixed_norm, grad_gain_two = norm_backward(mixed, inverse_two, gain_two, grad_normed_two)
    grad_mixed = out_grad[0].astype(f32) + grad_mixed_norm
    grad_attn = pair(grad_mixed.astype(bf16))
    grad_out_w = cols_from_rows(dot_tn(attended, grad_attn).astype(bf16))
    grad_attended = dot_nt(grad_attn, output_mat).astype(bf16)
    grad_out_w = chip_parts(grad_out_w)
    dq, dk, dv = attend_back(starts, cosine, sine, q_rot, k_rot, blended, grad_attended, length)
    grad_q, grad_k = (dot_tn(normed, d).astype(bf16) for d in (dq, dk))
    grad_q, grad_k, dq, dk, dv = tie((grad_q, grad_k, dq, dk, dv))
    grad_q, grad_k = chip_parts(grad_q), chip_parts(grad_k)
    grad_normed = mine_and_partner(
        dot_nt(dq, qkv_mat[:, :hw]) + dot_nt(dk, qkv_mat[:, hw : 2 * hw])
        + dot_nt(dv, qkv_mat[:, 2 * hw :])
    )
    grad_rows_norm, grad_gain_one = norm_backward(
        hidden[:length], inverse_one[:length], gain_one, grad_normed
    )
    input_grad = (grad_mixed + grad_rows_norm)[None]
    grad_first = in_order(dv[:length], swap(dv[length:]), 1)
    v1_grad_out = v1_grad_acc + grad_first.astype(f32)[None]

    rest = jnp.stack([square_first, square_blend])
    terms = []
    for _ in range(3):
        terms.append(lax.reduce_precision(rest, 8, 7))
        rest = rest - terms[-1]
    terms = jnp.concatenate([jnp.zeros((2,), f32)] + terms)
    row = lax.broadcasted_iota(jnp.int32, (width, 1), 0) % attn_gain.shape[0]
    extra = jnp.concatenate(
        [
            grad_gain_one[:, None], grad_gain_two[:, None],
            jnp.where(row == lax.axis_index("fsdp"), terms[None, 2:], 0.0),
        ],
        axis=1,
    )
    extra = jnp.pad(extra, ((0, 0), (0, LANES - extra.shape[1]))).astype(bf16)
    grad_v = dot_tn(normed, dv).astype(bf16)
    grad_a = jnp.concatenate([added(grad_q), added(grad_k), grad_v, extra], axis=1)
    grad_a, grad_b = tie((grad_a, grad_b))
    grad_b, grad_down, grad_out_w = tie((grad_b, grad_down, grad_out_w))
    grad_do = jnp.concatenate(
        [added(parts).reshape(fsdp, -1, hw // chips) for parts in (grad_down, grad_out_w)], axis=1
    )
    if by_ring:
        grad_do = grad_do.reshape(ring, 2, *grad_do.shape[1:])
        at_side = lambda which: lax.dynamic_slice_in_dim(grad_do, which, 1, 1)[:, 0]
        grad_do = added([at_side(side), sides(at_side(1 - side))])
        at_place = lambda step: lax.dynamic_slice_in_dim(grad_do, (place + step) % ring, 1, 0)[0]
        grad_do = added([at_place(0)] + [around(at_place(step), step) for step in range(1, ring)])
    else:
        grad_do = scatter(grad_do.reshape(-1, hw // chips))
    grad_a = scatter(row_major(grad_a))

    def from_chips(values):
        return [values] + [to_chip(values, step) for step in range(1, chips)]

    def whole_columns(half, other, at, size):
        return in_order(half[:, at : at + size], other[:, at : at + size], 1).astype(f32)

    ff_half = gate_mat.shape[1]
    half = added(from_chips(grad_b))
    other = swap(half)
    share_gate, share_up = (whole_columns(half, other, k * ff_half, ff_half) for k in range(2))
    def chip_order(got):
        return [
            functools.reduce(
                lambda kept, back: jnp.where((chip - back) % chips == which, got[back], kept),
                range(1, chips), got[0],
            )
            for which in range(chips)
        ]

    half = jnp.concatenate(chip_order(from_chips(grad_do)), axis=1)
    both = whole_columns(half, swap(half), 0, hw)
    share_down, share_output = both[: w_down.shape[0]], both[w_down.shape[0] :]
    got, share = from_chips(grad_a), hw // chips
    at_v = 2 * share
    half = jnp.concatenate(
        [
            piece for k in range(2)
            for piece in chip_order([g[:, k * share : (k + 1) * share] for g in got])
        ]
        + [added([g[:, at_v : at_v + hw] for g in got])]
        + [g[:, at_v + hw :] for g in got],
        axis=1,
    )
    other = swap(half)
    share_query, share_key, share_value = (
        whole_columns(half, other, k * hw, hw) for k in range(3)
    )
    gain_sums = sum(
        which[:, at : at + LANES].astype(f32)
        for which in (half, other) for at in range(3 * hw, half.shape[1], LANES)
    )
    share_gain_one, share_gain_two = gain_sums[:, 0], gain_sums[:, 1]
    squares = jnp.sum(gain_sums[:, 2:8], axis=0).reshape(3, 2).sum(axis=0)
    value_norms = jnp.sqrt(squares / f32(dp * fsdp * length * width))
    return (
        block_out, input_grad, share_gain_one, share_query, share_key, share_value, share_output,
        share_gain_two, share_gate, share_up, share_down, v1_grad_out, value_norms,
    )


def solution(mesh):
    tokens = ("dp", "fsdp")
    in_specs = (
        P(tokens, None, None), P(tokens, None, None), P(tokens, None), P("fsdp"),
        P("fsdp", None), P("fsdp", None), P("fsdp", None), P("fsdp", None), P("fsdp"),
        P("fsdp", None), P("fsdp", None), P("fsdp", None), P(tokens, None, None),
        P(tokens, None, None),
    )
    out_specs = (
        P(tokens, None, None), P(tokens, None, None), P("fsdp"), P("fsdp", None),
        P("fsdp", None), P("fsdp", None), P("fsdp", None), P("fsdp"), P("fsdp", None),
        P("fsdp", None), P("fsdp", None), P(tokens, None, None), P(),
    )
    return jax.shard_map(shards, mesh=mesh, in_specs=in_specs, out_specs=out_specs, check_vma=False)
```

```python
import functools
import math

import jax
import jax.numpy as jnp
from jax import lax
from jax.experimental import pallas as pl
from jax.experimental.layout import Layout, with_layout_constraint
from jax.experimental.pallas import tpu as pltpu
from jax.sharding import PartitionSpec as P

HEAD_DIM = 64
LANES = 128
REACH = 256
BLOCK = 128

eps_norm = 1e-06
rope_base = 10000.0
masked_score = -1e30
bf16 = jnp.bfloat16
f32 = jnp.float32


def positions_of(segment_ids):
    places = lax.broadcasted_iota(jnp.int32, segment_ids.shape, 1)
    before = jnp.concatenate([segment_ids[:, :1] - 1, segment_ids[:, :-1]], axis=1)
    starts = jnp.where(segment_ids != before, places, jnp.zeros_like(places))
    return places - lax.cummax(starts, axis=1)


def rope_tables(positions):
    half = HEAD_DIM // 2
    lane = lax.broadcasted_iota(jnp.int32, (1, LANES), 1)
    inverse = jnp.exp((lane % half).astype(f32) * (-math.log(rope_base) / half))
    angles = positions.astype(f32)[:, None] * inverse
    sign = jnp.where(lane % HEAD_DIM < half, -1.0, 1.0).astype(f32)
    return jnp.cos(angles), jnp.sin(angles) * sign


def halves_swapped(u):
    half = HEAD_DIM // 2
    lane = lax.broadcasted_iota(jnp.int32, u.shape, 1)
    return jnp.where(
        lane % HEAD_DIM < half, pltpu.roll(u, LANES - half, 1), pltpu.roll(u, half, 1)
    )


def head_lanes(u, head):
    lane = lax.broadcasted_iota(jnp.int32, u.shape, 1)
    return jnp.where(lane // HEAD_DIM == head, u, jnp.zeros_like(u))


def row_major(values):
    return with_layout_constraint(values, Layout(major_to_minor=(0, 1)))


def dot_nt(a, b):
    return lax.dot_general(a, b, (((1,), (1,)), ((), ())), preferred_element_type=f32)


def dot_tn(a, b):
    return lax.dot_general(a, b, (((0,), (0,)), ((), ())), preferred_element_type=f32)


def dot_nn(a, b):
    return jnp.dot(a, b, preferred_element_type=f32)


def softmax_block(q_head, k_rows, begin, first_key, starts):
    scores = dot_nt(q_head, k_rows) * (HEAD_DIM ** (-0.5))
    row = begin + lax.broadcasted_iota(jnp.int32, scores.shape, 0)
    col = first_key + lax.broadcasted_iota(jnp.int32, scores.shape, 1)
    allowed = (col <= row) & (col >= starts)
    scores = jnp.where(allowed, scores, masked_score)
    expo = jnp.exp(scores - jnp.max(scores, axis=1, keepdims=True))
    return expo / jnp.sum(expo, axis=1, keepdims=True)


def key_range(begin):
    return max(0, (begin - REACH + 1) // BLOCK * BLOCK), begin + BLOCK


def attend_kernel(
    start_ref, cos_ref, sin_ref, q_ref, k_ref, v_ref, first_ref,
    out_ref, q_rot_ref, k_rot_ref, blend_ref,
):
    cosine, sine = cos_ref[...], sin_ref[...]
    queries, keys = q_ref[...], k_ref[...]
    q_rot = (queries * cosine + halves_swapped(queries) * sine).astype(bf16)
    k_rot = (keys * cosine + halves_swapped(keys) * sine).astype(bf16)
    blended = (0.5 * v_ref[...] + 0.5 * first_ref[...].astype(f32)).astype(bf16)
    q_rot_ref[...] = q_rot
    k_rot_ref[...] = k_rot
    blend_ref[...] = blended
    for begin in range(0, q_rot.shape[0], BLOCK):
        low, high = key_range(begin)
        starts = start_ref[begin : begin + BLOCK, :]
        total = jnp.zeros((BLOCK, LANES), f32)
        for head in range(LANES // HEAD_DIM):
            q_head = head_lanes(q_rot[begin : begin + BLOCK, :], head)
            probs = softmax_block(q_head, k_rot[low:high, :], begin, low, starts)
            total = total + dot_nn(probs.astype(bf16), head_lanes(blended[low:high, :], head))
        out_ref[begin : begin + BLOCK, :] = total.astype(bf16)


def attend_back_kernel(
    start_ref, cos_ref, sin_ref, q_rot_ref, k_rot_ref, blend_ref, grad_ref,
    dq_ref, dk_ref, dv_ref, dk_sum, dv_sum,
):
    scale = HEAD_DIM ** (-0.5)
    cosine, sine = cos_ref[...], sin_ref[...]
    q_rot, k_rot, blended, grads = q_rot_ref[...], k_rot_ref[...], blend_ref[...], grad_ref[...]
    dk_sum[...] = jnp.zeros_like(dk_sum)
    dv_sum[...] = jnp.zeros_like(dv_sum)
    for begin in range(0, q_rot.shape[0], BLOCK):
        low, high = key_range(begin)
        rows = slice(begin, begin + BLOCK)
        starts = start_ref[rows, :]
        dq = jnp.zeros((BLOCK, LANES), f32)
        for head in range(LANES // HEAD_DIM):
            q_head = head_lanes(q_rot[rows, :], head)
            k_head = head_lanes(k_rot[low:high, :], head)
            g_head = head_lanes(grads[rows, :], head)
            probs = softmax_block(q_head, k_rot[low:high, :], begin, low, starts)
            grad_probs = dot_nt(g_head, blended[low:high, :])
            inner = jnp.sum(probs * grad_probs, axis=1, keepdims=True)
            grad_scores = (probs * (grad_probs - inner)).astype(bf16)
            dq = dq + dot_nn(grad_scores, k_head)
            dk_sum[low:high, :] += dot_tn(grad_scores, q_head)
            dv_sum[low:high, :] += dot_tn(probs.astype(bf16), g_head)
        dq = dq * scale
        dq_ref[rows, :] = (
            dq * cosine[rows, :] - halves_swapped(dq) * sine[rows, :]
        ).astype(bf16)
    dk = dk_sum[...] * scale
    dk_ref[...] = (dk * cosine - halves_swapped(dk) * sine).astype(bf16)
    dv_ref[...] = (0.5 * dv_sum[...]).astype(bf16)


def attend(starts, cosine, sine, qkv, first, length):
    tokens, width = first.shape
    pairs = width // LANES
    per_row = lambda lanes: pl.BlockSpec((length, lanes), lambda r, h: (r, 0))
    part = lambda k: pl.BlockSpec((length, LANES), lambda r, h: (r, k * pairs + h))
    return pl.pallas_call(
        attend_kernel,
        grid=(tokens // length, pairs),
        in_specs=[per_row(1), per_row(LANES), per_row(LANES), part(0), part(1), part(2), part(0)],
        out_specs=[part(0)] * 4,
        out_shape=[jax.ShapeDtypeStruct((tokens, width), bf16)] * 4,
        name="attend",
    )(starts, cosine, sine, qkv, qkv, qkv, first)


def attend_back(starts, cosine, sine, q_rot, k_rot, blended, grads, length):
    tokens, width = grads.shape
    per_row = lambda lanes: pl.BlockSpec((length, lanes), lambda r, h: (r, 0))
    part = pl.BlockSpec((length, LANES), lambda r, h: (r, h))
    return pl.pallas_call(
        attend_back_kernel,
        grid=(tokens // length, width // LANES),
        in_specs=[per_row(1), per_row(LANES), per_row(LANES)] + [part] * 4,
        out_specs=[part] * 3,
        out_shape=[jax.ShapeDtypeStruct((tokens, width), bf16)] * 3,
        scratch_shapes=[pltpu.VMEM((length, LANES), f32)] * 2,
        name="attend_back",
    )(starts, cosine, sine, q_rot, k_rot, blended, grads)


def order_kernel(at_ref, *refs):
    *pieces, out_ref = refs
    count = len(pieces)
    for step, piece in enumerate(pieces):
        out_ref[lax.rem(at_ref[0] + count - step, count)] = piece[...]


def in_ring_order(place, pieces):
    in_vmem = pl.BlockSpec(memory_space=pltpu.VMEM)
    return pl.pallas_call(
        order_kernel,
        in_specs=[pl.BlockSpec(memory_space=pltpu.SMEM)] + [in_vmem] * len(pieces),
        out_specs=in_vmem,
        out_shape=jax.ShapeDtypeStruct((len(pieces),) + pieces[0].shape, pieces[0].dtype),
        name="ring_order",
    )(jnp.stack([place]), *pieces)


def join_kernel(at_ref, mine_ref, far_ref, mine_other_ref, far_other_ref, out_ref):
    size = mine_other_ref.shape[2]
    shared = mine_ref.shape[2] - size
    side, chip = at_ref[0], at_ref[1]
    for own, other_ref, row in (
        (mine_ref, mine_other_ref, side), (far_ref, far_other_ref, 1 - side)
    ):
        if shared:
            out_ref[:, row, :, :shared] = own[:, :, :shared]
        for which in range(2):
            @pl.when(chip == which)
            def _():
                first, second = shared + which * size, shared + (1 - which) * size
                out_ref[:, row, :, first : first + size] = own[:, :, shared:]
                out_ref[:, row, :, second : second + size] = other_ref[...]


def joined(side, chip, mine, far, mine_other, far_other):
    ring, height, held = mine.shape
    in_vmem = pl.BlockSpec(memory_space=pltpu.VMEM)
    full = jax.ShapeDtypeStruct((ring, 2, height, held + mine_other.shape[2]), mine.dtype)
    whole = pl.pallas_call(
        join_kernel,
        in_specs=[pl.BlockSpec(memory_space=pltpu.SMEM)] + [in_vmem] * 4,
        out_specs=in_vmem,
        out_shape=full,
        name="joined",
    )(jnp.stack([side, chip]), mine, far, mine_other, far_other)
    return whole.reshape(ring * 2 * height, full.shape[3])


def norm_stats(values):
    return lax.rsqrt(jnp.mean(values * values, axis=-1, keepdims=True) + eps_norm)


def norm_backward(values, inverse, gain_f, grad_out):
    scaled = values * inverse
    grad_scaled = grad_out * gain_f
    grad_gain = jnp.sum(grad_out * scaled, axis=0)
    grad_values = inverse * (
        grad_scaled - scaled * jnp.mean(grad_scaled * scaled, axis=-1, keepdims=True)
    )
    return grad_values, grad_gain


def shards(
    hidden_in, value_first, segment_ids, attn_gain, w_query, w_key, w_value, w_output,
    mlp_gain, w_gate, w_up, w_down, out_grad, v1_grad_acc,
):
    length, width = hidden_in.shape[1:]
    dp, fsdp = lax.axis_size("dp"), lax.axis_size("fsdp")
    core, chip = lax.axis_index("dp") % 2, lax.axis_index("dp") // 2
    chips = dp // 2
    hw = width // 2

    def swap(values):
        return lax.ppermute(values, "dp", [(i, i ^ 1) for i in range(dp)])

    def to_chip(values, step):
        return lax.ppermute(values, "dp", [(i, (i + 2 * step) % dp) for i in range(dp)])

    def part(values, which):
        share = values.shape[-1] // chips
        return lax.dynamic_slice_in_dim(values, which * share, share, values.ndim - 1)

    def chip_parts(values):
        return [part(values, chip)] + [
            to_chip(part(values, (chip + step) % chips), step) for step in range(1, chips)
        ]

    def added(parts):
        return sum(p.astype(f32) for p in parts).astype(bf16)

    def pair(values):
        return jnp.concatenate([values, swap(values)], axis=0)

    def cols(values, which):
        half = values.shape[-1] // 2
        return lax.dynamic_slice_in_dim(values, which * half, half, values.ndim - 1)

    def rows(values, which):
        half = values.shape[0] // 2
        return lax.dynamic_slice_in_dim(values, which * half, half, 0)

    def in_order(mine, other, axis):
        return jnp.concatenate(
            [jnp.where(core == 0, mine, other), jnp.where(core == 0, other, mine)], axis=axis
        )

    def rows_from_cols(mine):
        return in_order(rows(mine, core), swap(rows(mine, 1 - core)), 1)

    def cols_from_rows(mine):
        return in_order(cols(mine, core), swap(cols(mine, 1 - core)), 0)

    def gather(shard):
        return lax.all_gather(shard, "fsdp", axis=0, tiled=True)

    def scatter(whole):
        return lax.psum_scatter(whole, "fsdp", scatter_dimension=0, tiled=True)

    ring, place = fsdp // 2, lax.axis_index("fsdp") // 2
    side = lax.axis_index("fsdp") % 2

    def sides(values):
        return lax.ppermute(values, "fsdp", [(i, i ^ 1) for i in range(fsdp)])

    def around(values, step):
        return lax.ppermute(values, "fsdp", [(i, (i + 2 * step) % fsdp) for i in range(fsdp)])

    def shared_lanes(shard):
        lanes = shard.shape[1] // LANES
        return (lanes - 2 * (lanes // 2)) * LANES

    def held_columns(shard):
        shared = shared_lanes(shard)
        size = (shard.shape[1] - shared) // 2
        held = lax.dynamic_slice_in_dim(shard, shared + chip * size, size, 1)
        return jnp.concatenate([shard[:, :shared], held], axis=1) if shared else held

    def ring_pieces(held):
        return [held] + [around(held, step) for step in range(1, ring)]

    def half_of(shard, values):
        return values[:, :, shared_lanes(shard) :]

    def mine_and_partner(partial):
        return partial[:length] + swap(partial[length:].astype(bf16)).astype(f32)

    gains = jnp.stack([attn_gain, mlp_gain])
    gains = jnp.pad(gains, ((0, w_query.shape[0] - 2), (0, max(0, LANES - gains.shape[1]))))
    by_ring, tie = chips == 2 and fsdp <= 8, lax.optimization_barrier
    shard_a = jnp.concatenate([gains] + [cols(w, core) for w in (w_query, w_key, w_value)], axis=1)
    shard_b = jnp.concatenate([cols(w_output, core), cols(w_gate, core)], axis=1)
    height, down_height = w_query.shape[0], w_down.shape[0]
    blocks = -(-down_height // height)
    shard_d = jnp.pad(cols(w_down, core), ((0, blocks * height - down_height), (0, 0)))
    shard_c = jnp.concatenate(
        [cols(w_up, core)] + [shard_d[k * height : (k + 1) * height] for k in range(blocks)], axis=1
    )
    if by_ring:
        join = functools.partial(joined, side, chip)
        pieces_a = ring_pieces(held_columns(shard_a))
        pieces_a, held_b = tie((pieces_a, held_columns(shard_b)))
        pieces_b = ring_pieces(held_b)
        mine_a = in_ring_order(place, pieces_a)
        mine_a, half_a = tie((mine_a, half_of(shard_a, mine_a)))
        far_a, mine_other_a = sides(mine_a), to_chip(half_a, 1)
        pieces_b, far_a, mine_a, mine_other_a, shard_c = tie(
            (pieces_b, far_a, mine_a, mine_other_a, shard_c)
        )
        half_a = half_of(shard_a, far_a)
        mine_b = in_ring_order(place, pieces_b)
        half_a, mine_b, half_b = tie((half_a, mine_b, half_of(shard_b, mine_b)))
        far_other_a, far_b, mine_other_b = to_chip(half_a, 1), sides(mine_b), to_chip(half_b, 1)
        whole_a = join(mine_a, far_a, mine_other_a, far_other_a)
    else:
        whole_a = gather(shard_a)
    whole_c = gather(shard_c)
    qkv_mat = whole_a[:, gains.shape[1] :]
    gain_rows = whole_a[:, : gains.shape[1]].reshape(fsdp, w_query.shape[0], -1)
    gain_one = gain_rows[:, 0, : attn_gain.shape[0]].reshape(1, width).astype(f32)
    gain_two = gain_rows[:, 1, : attn_gain.shape[0]].reshape(1, width).astype(f32)

    segments = pair(segment_ids)
    positions = positions_of(segments)
    starts = (lax.broadcasted_iota(jnp.int32, positions.shape, 1) - positions).reshape(-1, 1)
    cosine, sine = rope_tables(positions.reshape(-1))
    hidden = pair(hidden_in[0]).astype(f32)
    first = value_first[0]
    first_half = jnp.concatenate([cols(first, core), swap(cols(first, 1 - core))], axis=0)
    cotangent = pair(out_grad[0])

    inverse_one = norm_stats(hidden)
    normed = (hidden * inverse_one * gain_one).astype(bf16)
    qkv = dot_nn(normed, qkv_mat)
    if by_ring:
        far_b, qkv = tie((far_b, qkv))
        half_b, qkv = tie((half_of(shard_b, far_b), qkv))
        far_other_b = to_chip(half_b, 1)
    attended, q_rot, k_rot, blended = attend(starts, cosine, sine, qkv, first_half, length)
    if by_ring:
        attended, far_b, mine_other_b, far_other_b = tie(
            (attended, far_b, mine_other_b, far_other_b)
        )
        whole_b = join(mine_b, far_b, mine_other_b, far_other_b)
    else:
        whole_b = gather(shard_b)
    output_mat, gate_mat = rows_from_cols(whole_b[:, :hw]), whole_b[:, hw:]
    first_f, blended_f = first.astype(f32), blended.astype(f32)
    square_first, square_blend = jnp.sum(first_f * first_f), jnp.sum(blended_f * blended_f)

    mixed = hidden[:length] + mine_and_partner(dot_nn(attended, output_mat))
    inverse_two = norm_stats(mixed)
    normed_two = pair((mixed * inverse_two * gain_two).astype(bf16))
    normed_two, whole_c, square_first, square_blend = tie(
        (normed_two, whole_c, square_first, square_blend)
    )
    up_mat, whole_d = whole_c[:, : w_up.shape[1] // 2], whole_c[:, w_up.shape[1] // 2 :]
    gate = dot_nn(normed_two, gate_mat)
    up_val = dot_nn(normed_two, up_mat)

    def unpacked(packed):
        stacked = jnp.concatenate(
            [packed[:, k * hw : (k + 1) * hw].reshape(-1, height, hw) for k in range(blocks)], axis=1
        )
        return stacked[:, :down_height].reshape(-1, hw)

    down_mat = in_order(unpacked(rows(whole_d, core)), unpacked(swap(rows(whole_d, 1 - core))), 1)
    sigma = jax.nn.sigmoid(gate)
    silu_gate = gate * sigma
    act = (silu_gate * up_val).astype(bf16)
    block_out = (mixed + mine_and_partner(dot_nn(act, down_mat))).astype(bf16)[None]

    grad_act = dot_nt(cotangent, down_mat)
    grad_gate = (grad_act * up_val * sigma * (1.0 + gate * (1.0 - sigma))).astype(bf16)
    grad_upv = (grad_act * silu_gate).astype(bf16)
    grad_b = jnp.concatenate(
        [dot_tn(normed_two, grad_gate).astype(bf16), dot_tn(normed_two, grad_upv).astype(bf16)],
        axis=1,
    )
    grad_b, act, grad_gate, grad_upv = tie((grad_b, act, grad_gate, grad_upv))
    grad_b = scatter(grad_b)
    grad_down = chip_parts(cols_from_rows(dot_tn(act, cotangent).astype(bf16)))
    grad_normed_two = mine_and_partner(
        dot_nt(grad_gate, gate_mat) + dot_nt(grad_upv, up_mat)
    )
    grad_mixed_norm, grad_gain_two = norm_backward(mixed, inverse_two, gain_two, grad_normed_two)
    grad_mixed = out_grad[0].astype(f32) + grad_mixed_norm
    grad_attn = pair(grad_mixed.astype(bf16))
    grad_out_w = cols_from_rows(dot_tn(attended, grad_attn).astype(bf16))
    grad_attended = dot_nt(grad_attn, output_mat).astype(bf16)
    grad_out_w = chip_parts(grad_out_w)
    dq, dk, dv = attend_back(starts, cosine, sine, q_rot, k_rot, blended, grad_attended, length)
    grad_q, grad_k = (dot_tn(normed, d).astype(bf16) for d in (dq, dk))
    grad_q, grad_k, dq, dk, dv = tie((grad_q, grad_k, dq, dk, dv))
    grad_q, grad_k = chip_parts(grad_q), chip_parts(grad_k)
    grad_normed = mine_and_partner(
        dot_nt(dq, qkv_mat[:, :hw]) + dot_nt(dk, qkv_mat[:, hw : 2 * hw])
        + dot_nt(dv, qkv_mat[:, 2 * hw :])
    )
    grad_rows_norm, grad_gain_one = norm_backward(
        hidden[:length], inverse_one[:length], gain_one, grad_normed
    )
    input_grad = (grad_mixed + grad_rows_norm)[None]
    grad_first = in_order(dv[:length], swap(dv[length:]), 1)
    v1_grad_out = v1_grad_acc + grad_first.astype(f32)[None]

    rest = jnp.stack([square_first, square_blend])
    terms = []
    for _ in range(3):
        terms.append(lax.reduce_precision(rest, 8, 7))
        rest = rest - terms[-1]
    terms = jnp.concatenate([jnp.zeros((2,), f32)] + terms)
    row = lax.broadcasted_iota(jnp.int32, (width, 1), 0) % attn_gain.shape[0]
    extra = jnp.concatenate(
        [
            grad_gain_one[:, None], grad_gain_two[:, None],
            jnp.where(row == lax.axis_index("fsdp"), terms[None, 2:], 0.0),
        ],
        axis=1,
    )
    extra = jnp.pad(extra, ((0, 0), (0, LANES - extra.shape[1]))).astype(bf16)
    grad_v = dot_tn(normed, dv).astype(bf16)
    grad_a = jnp.concatenate([added(grad_q), added(grad_k), grad_v, extra], axis=1)
    grad_a, grad_b = tie((grad_a, grad_b))
    grad_b, grad_down, grad_out_w = tie((grad_b, grad_down, grad_out_w))
    grad_do = jnp.concatenate(
        [added(parts).reshape(fsdp, -1, hw // chips) for parts in (grad_down, grad_out_w)], axis=1
    )
    if by_ring:
        grad_do = grad_do.reshape(ring, 2, *grad_do.shape[1:])
        at_side = lambda which: lax.dynamic_slice_in_dim(grad_do, which, 1, 1)[:, 0]
        grad_do = added([at_side(side), sides(at_side(1 - side))])
        at_place = lambda step: lax.dynamic_slice_in_dim(grad_do, (place + step) % ring, 1, 0)[0]
        grad_do = added([at_place(0)] + [around(at_place(step), step) for step in range(1, ring)])
    else:
        grad_do = scatter(grad_do.reshape(-1, hw // chips))
    grad_a = scatter(row_major(grad_a))

    def from_chips(values):
        return [values] + [to_chip(values, step) for step in range(1, chips)]

    def whole_columns(half, other, at, size):
        return in_order(half[:, at : at + size], other[:, at : at + size], 1).astype(f32)

    ff_half = gate_mat.shape[1]
    half = added(from_chips(grad_b))
    other = swap(half)
    share_gate, share_up = (whole_columns(half, other, k * ff_half, ff_half) for k in range(2))
    def chip_order(got):
        return [
            functools.reduce(
                lambda kept, back: jnp.where((chip - back) % chips == which, got[back], kept),
                range(1, chips), got[0],
            )
            for which in range(chips)
        ]

    half = jnp.concatenate(chip_order(from_chips(grad_do)), axis=1)
    both = whole_columns(half, swap(half), 0, hw)
    share_down, share_output = both[: w_down.shape[0]], both[w_down.shape[0] :]
    got, share = from_chips(grad_a), hw // chips
    at_v = 2 * share
    half = jnp.concatenate(
        [
            piece for k in range(2)
            for piece in chip_order([g[:, k * share : (k + 1) * share] for g in got])
        ]
        + [added([g[:, at_v : at_v + hw] for g in got])]
        + [g[:, at_v + hw :] for g in got],
        axis=1,
    )
    other = swap(half)
    share_query, share_key, share_value = (
        whole_columns(half, other, k * hw, hw) for k in range(3)
    )
    gain_sums = sum(
        which[:, at : at + LANES].astype(f32)
        for which in (half, other) for at in range(3 * hw, half.shape[1], LANES)
    )
    share_gain_one, share_gain_two = gain_sums[:, 0], gain_sums[:, 1]
    squares = jnp.sum(gain_sums[:, 2:8], axis=0).reshape(3, 2).sum(axis=0)
    value_norms = jnp.sqrt(squares / f32(dp * fsdp * length * width))
    return (
        block_out, input_grad, share_gain_one, share_query, share_key, share_value, share_output,
        share_gain_two, share_gate, share_up, share_down, v1_grad_out, value_norms,
    )


def solution(mesh):
    tokens = ("dp", "fsdp")
    in_specs = (
        P(tokens, None, None), P(tokens, None, None), P(tokens, None), P("fsdp"),
        P("fsdp", None), P("fsdp", None), P("fsdp", None), P("fsdp", None), P("fsdp"),
        P("fsdp", None), P("fsdp", None), P("fsdp", None), P(tokens, None, None),
        P(tokens, None, None),
    )
    out_specs = (
        P(tokens, None, None), P(tokens, None, None), P("fsdp"), P("fsdp", None),
        P("fsdp", None), P("fsdp", None), P("fsdp", None), P("fsdp"), P("fsdp", None),
        P("fsdp", None), P("fsdp", None), P(tokens, None, None), P(),
    )
    return jax.shard_map(shards, mesh=mesh, in_specs=in_specs, out_specs=out_specs, check_vma=False)
```
